128 devices in a mesh: lat: 4 (over y_lo, core), lon: 32 (over z, y_hi, x).
Axes of the slice: x: 4, y: 4 (y_hi: 2, y_lo: 2; y = y_hi * 2 + y_lo), z: 4, core: 2. Of those that a mesh axis runs over, the one named last changes fastest.
Arguments:
- inputs: bfloat16 [2, 192, 64, 4096], P(None, None, 'lat', 'lon'), may hold values from -6 to 6
- cotangent: bfloat16 [2, 192, 64, 4096], P(None, None, 'lat', 'lon'), may hold values from -6 to 6
- kernel: float32 [192, 7, 7], replicated, may hold values from -0.875 to 0.875
- conv_bias: float32 [192], replicated, may hold values from -3 to 3
- norm_gain: float32 [192], replicated, may hold values from 0.5 to 1.5
- norm_bias: float32 [192], replicated, may hold values from -3 to 3
- w_in: bfloat16 [192, 768], replicated, may hold values from -0.4375 to 0.4375
- bias_in: float32 [768], replicated, may hold values from -3 to 3
- w_out: bfloat16 [768, 192], replicated, may hold values from -0.21875 to 0.21875
- bias_out: float32 [192], replicated, may hold values from -3 to 3
- layer_scale: float32 [192], replicated, may hold values from 0.5 to 1.5
Outputs:
- output: bfloat16 [2, 192, 64, 4096], P(None, None, 'lat', 'lon')
- grad_input: bfloat16 [2, 192, 64, 4096], P(None, None, 'lat', 'lon')
- grad_kernel: float32 [192, 7, 7], replicated
- grad_w_in: float32 [192, 768], replicated
- grad_w_out: float32 [768, 192], replicated
The draws below stay inside these ranges and needn't reach their ends.
All inputs are finite; a program needn't handle non-finite values.
Results may differ from the reference program's by a relative error of at most 0.0068.
Values may be sent and summed in bfloat16 or wider, within the bound.
No kernel may reach another device: no remote copies, remote signals or barrier semaphores. Data moves between devices by JAX's collectives and lax.ppermute only.
A program may use at most 128 MiB of HBM per device.

```python
import math
import jax
import jax.numpy as jnp
from jax import lax

C = 192
HID = 768
KSIZE = 7
MEMBERS = 2
LAT_DEV = 16
NLAT = 64
NLON = 4096
N_LAT = 4


def levels(stream_key, extent, shards, smallest, top_value):
    def one(dim, shards_of):
        heights = jax.random.uniform(jax.random.fold_in(jax.random.fold_in(stream_key, 6), dim), (shards_of,), jnp.float32, smallest / len(shards), top_value / len(shards))
        return jnp.repeat(jnp.exp(heights), extent[dim] // shards_of).reshape((-1,) + (1,) * (len(extent) - dim - 1))

    loudness = one(*shards[0])
    for cut in shards[1:]:
        loudness = loudness * one(*cut)
    return loudness


def normal_values(stream_key, extent, width, most, pieces=(), held_as=jnp.bfloat16):
    values = jax.random.normal(stream_key, extent, jnp.float32) * width
    if len(pieces) > 0:
        values = levels(stream_key, extent, pieces, -0.22, 0.18) * values
    return jnp.clip(values, min=-most, max=most).astype(held_as)


def setup_inputs(seed: int = 0) -> dict:
    key_of = jax.random.split(jax.random.key(seed), 12)
    inputs = normal_values(key_of[0], (MEMBERS, C, NLAT, NLON), 1.0, 6.0, ((2, 4), (3, 32)))
    cotangent = normal_values(key_of[1], (MEMBERS, C, NLAT, NLON), 1.0, 6.0, ((2, 4), (3, 32)))
    kernel = normal_values(key_of[2], (C, KSIZE, KSIZE), (KSIZE * KSIZE) ** -0.5, 0.875, (), jnp.float32)
    conv_bias = normal_values(key_of[3], (C,), 0.5, 3.0, (), jnp.float32)
    norm_gain = jnp.clip(jax.random.uniform(key_of[4], (C,), jnp.float32, 0.5, 1.5), 0.5, 1.5)
    norm_bias = normal_values(key_of[5], (C,), 0.5, 3.0, (), jnp.float32)
    w_in = normal_values(key_of[6], (C, HID), C ** -0.5, 0.4375)
    bias_in = normal_values(key_of[7], (HID,), 0.5, 3.0, (), jnp.float32)
    w_out = normal_values(key_of[8], (HID, C), HID ** -0.5, 0.21875)
    bias_out = normal_values(key_of[9], (C,), 0.5, 3.0, (), jnp.float32)
    layer_scale = jnp.clip(jax.random.uniform(key_of[10], (C,), jnp.float32, 0.5, 1.5), 0.5, 1.5)
    return dict(inputs=inputs, cotangent=cotangent, kernel=kernel, conv_bias=conv_bias, norm_gain=norm_gain, norm_bias=norm_bias, w_in=w_in, bias_in=bias_in, w_out=w_out, bias_out=bias_out, layer_scale=layer_scale)


eps_norm = 1e-06
inv_root_two = 0.7071067811865476
inv_root_tau = 0.3989422804014327

def fold_pad(values, margin):
    half_turn = values.shape[3] // 2
    north_rows = jnp.flip(jnp.roll(values[:, :, :margin], half_turn, axis=3), axis=2)
    south_rows = jnp.flip(jnp.roll(values[:, :, -margin:], half_turn, axis=3), axis=2)
    stacked = jnp.concatenate([north_rows, values, south_rows], axis=2)
    return jnp.concatenate([stacked[..., -margin:], stacked, stacked[..., :margin]], axis=3)

def depthwise(padded, kernel):
    return lax.conv_general_dilated(padded, kernel[:, None], (1, 1), 'VALID', dimension_numbers=('NCHW', 'OIHW', 'NCHW'), feature_group_count=kernel.shape[0], precision=lax.Precision.HIGHEST)

def gelu_slope(pre_act):
    return 0.5 * (1.0 + jax.scipy.special.erf(pre_act * inv_root_two)) + pre_act * jnp.exp(-0.5 * pre_act * pre_act) * inv_root_tau

def block_math(band_block, band_cot, kernel, conv_bias, norm_gain, norm_bias, w_in, bias_in, w_out, bias_out, layer_scale):
    members, channels, height, breadth = band_cot.shape
    wide_block = band_block.astype(jnp.float32)
    conv_out = depthwise(wide_block, kernel) + conv_bias[None, :, None, None]
    centred = conv_out - lax.optimization_barrier(jnp.mean(conv_out, axis=1, keepdims=True))
    inv_std = lax.rsqrt(lax.optimization_barrier(jnp.mean(centred * centred, axis=1, keepdims=True)) + eps_norm)
    x_hat = centred * inv_std
    normed = (x_hat * norm_gain[None, :, None, None] + norm_bias[None, :, None, None]).astype(jnp.bfloat16)
    normed_wide = normed.reshape(members, channels, height * breadth).astype(jnp.float32)
    w_in_wide = w_in.astype(jnp.float32)
    w_out_wide = w_out.astype(jnp.float32)
    highest = lax.Precision.HIGHEST
    pre_act = jnp.einsum('ch,bcn->bhn', w_in_wide, normed_wide, precision=highest) + bias_in[None, :, None]
    act_round = jax.nn.gelu(pre_act, approximate=False).astype(jnp.bfloat16)
    act_wide = act_round.astype(jnp.float32)
    mlp_out = jnp.einsum('hc,bhn->bcn', w_out_wide, act_wide, precision=highest) + bias_out[None, :, None]
    scale_col = layer_scale[None, :, None]
    residual = band_block[:, :, 3:-3, 3:-3].reshape(members, channels, height * breadth)
    output = (residual.astype(jnp.float32) + scale_col * mlp_out).astype(jnp.bfloat16).reshape(members, channels, height, breadth)
    g_mlp = (scale_col * band_cot.reshape(members, channels, height * breadth).astype(jnp.float32)).astype(jnp.bfloat16)
    g_mlp_wide = g_mlp.astype(jnp.float32)
    grad_out = jnp.einsum('bhn,bcn->hc', act_wide, g_mlp_wide, precision=highest)
    g_act = jnp.einsum('hc,bcn->bhn', w_out_wide, g_mlp_wide, precision=highest)
    g_pre = (g_act * gelu_slope(pre_act)).astype(jnp.bfloat16)
    g_pre_wide = g_pre.astype(jnp.float32)
    grad_in = jnp.einsum('bcn,bhn->ch', normed_wide, g_pre_wide, precision=highest)
    g_norm = jnp.einsum('ch,bhn->bcn', w_in_wide, g_pre_wide, precision=highest).reshape(members, channels, height, breadth)
    g_hat = g_norm * norm_gain[None, :, None, None]
    g_conv = inv_std * (g_hat - lax.optimization_barrier(jnp.mean(g_hat, axis=1, keepdims=True)) - x_hat * lax.optimization_barrier(jnp.mean(g_hat * x_hat, axis=1, keepdims=True)))
    g_round = g_conv.astype(jnp.bfloat16)
    g_wide = lax.optimization_barrier(g_round).astype(jnp.float32)
    kernel_taps = []
    for row_off in range(KSIZE):
        for col_off in range(KSIZE):
            kernel_taps.append(lax.optimization_barrier(jnp.sum(g_wide * wide_block[:, :, row_off:row_off + height, col_off:col_off + breadth], axis=(0, 2, 3))))
    grad_kernel = jnp.stack(kernel_taps, axis=1).reshape(channels, KSIZE, KSIZE)
    return (output, g_round, grad_in, grad_out, grad_kernel)

def reference(inputs, cotangent, kernel, conv_bias, norm_gain, norm_bias, w_in, bias_in, w_out, bias_out, layer_scale):
    half_span = KSIZE // 2
    lat_cells = inputs.shape[2]
    lon_cells = inputs.shape[3]
    padded = fold_pad(inputs, half_span)
    anchor = jnp.zeros((), jnp.int32)

    def band_step(totals, step_index):
        member = (step_index // N_LAT).astype(jnp.int32)
        row_start = (step_index % N_LAT * LAT_DEV).astype(jnp.int32)
        band_block = lax.dynamic_slice(padded, (member, anchor, row_start, anchor), (1, C, LAT_DEV + 2 * half_span, lon_cells + 2 * half_span))
        band_cot = lax.dynamic_slice(cotangent, (member, anchor, row_start, anchor), (1, C, LAT_DEV, lon_cells))
        output, g_round, grad_in, grad_out, grad_kernel = block_math(band_block, band_cot, kernel, conv_bias, norm_gain, norm_bias, w_in, bias_in, w_out, bias_out, layer_scale)
        return ((totals[0] + grad_in, totals[1] + grad_out, totals[2] + grad_kernel), (output[0], g_round[0]))
    start_totals = (jnp.zeros((C, HID), jnp.float32), jnp.zeros((HID, C), jnp.float32), jnp.zeros((C, KSIZE, KSIZE), jnp.float32))
    totals, (out_bands, grad_bands) = lax.scan(band_step, start_totals, jnp.arange(MEMBERS * N_LAT, dtype=jnp.int32))

    def unband(bands):
        return bands.reshape(MEMBERS, N_LAT, C, LAT_DEV, lon_cells).transpose(0, 2, 1, 3, 4).reshape(MEMBERS, C, lat_cells, lon_cells)
    output = unband(out_bands)
    g_full = unband(grad_bands)

    def spread_map(values):
        return depthwise(fold_pad(values, half_span), kernel)
    back_parts = []
    for member in range(MEMBERS):
        primal, pullback = jax.vjp(spread_map, inputs[member:member + 1].astype(jnp.float32))
        back_parts.append(pullback(g_full[member:member + 1].astype(jnp.float32))[0])
    grad_input = (cotangent.astype(jnp.float32) + jnp.concatenate(back_parts, axis=0)).astype(jnp.bfloat16)
    factor = 1.0 / math.sqrt(MEMBERS * lat_cells * lon_cells)
    return (output, grad_input, totals[2] * factor, totals[0] * factor, totals[1] * factor)
```

```python
import math

import jax
import jax.numpy as jnp
import numpy as np
from jax import lax
from jax.experimental import pallas as pl
from jax.experimental.pallas import tpu as pltpu
from jax.sharding import PartitionSpec as P

eps_norm = 1e-06
inv_root_two = 0.7071067811865476
inv_root_tau = 0.3989422804014327
f32 = jnp.float32
bf16 = jnp.bfloat16

M, C, HID, ROWS, LON = 2, 192, 768, 16, 128
GROUP = 32
NG = C // GROUP
TAPS = 7
N_LAT, N_LON = 4, 32
CELLS = 256
CHUNK_ROWS = 24
FLAT = 128 * CHUNK_ROWS
PARAMS = pltpu.CompilerParams(vmem_limit_bytes=60 * 2**20)


def halo_row(lat, pos):
    half, k = divmod(pos, 4)
    if half > 1:
        return 99
    if lat == 0:
        return 16 + k if half == 0 else -1 - k
    if lat == 1:
        return k - 4 if half == 0 else 16 + k
    if lat == 2:
        return 16 + k if half == 0 else k - 4
    return k - 4 if half == 0 else 19 - k


def tap_tables():
    fwd = np.full((N_LAT, ROWS, 256), 127, np.int32)
    spr = np.full((N_LAT, ROWS, 256), 127, np.int32)
    diag = np.zeros((N_LAT, 2, ROWS, 128), np.int32)
    for lat in range(N_LAT):
        for i in range(ROWS):
            for pos in range(32):
                k = pos % 4
                row = pos - 16 if pos >= 16 else halo_row(lat, pos)
                a_fwd = row - i + 3
                a_spr = i - row + 3
                if lat == 0 and 4 <= pos < 8:
                    a_spr = 2 - i - k
                if lat == 3 and 4 <= pos < 8:
                    a_spr = 22 - i - k
                for t in range(TAPS):
                    if 0 <= a_fwd < TAPS:
                        fwd[lat, i, t * 32 + pos] = t * 8 + a_fwd
                        half, lane = (0, t * 8) if t < 4 else (1, t * 8)
                        diag[lat, half, i, lane + a_fwd] = (t % 4) * 32 + pos
                    if 0 <= a_spr < TAPS:
                        spr[lat, i, t * 32 + pos] = (6 - t) * 8 + a_spr
    return fwd, spr, diag


FWD_TABLE, SPR_TABLE, DIAG_TABLE = tap_tables()


def pick(cc, transposed):
    shape = (128, 256) if transposed else (256, 128)
    packed = lax.broadcasted_iota(jnp.int32, shape, 1 if transposed else 0)
    lane = lax.broadcasted_iota(jnp.int32, shape, 0 if transposed else 1)
    k = packed % 128 - 4 * cc
    hit = (k >= 0) & (k < 3) & (lane == k + jnp.where(packed < 128, 125, 0))
    return jnp.where(hit, 1.0, 0.0).astype(bf16)


def maps_kernel(vec, bias, vecs, bias_wide, to_pack, to_edge):
    columns = jnp.transpose(vec[...])
    for k in range(5):
        vecs[k] = jnp.broadcast_to(columns[:, k : k + 1], (C, 128))
    columns = jnp.transpose(bias[...])
    bias_wide[...] = jnp.broadcast_to(columns[:, 0:1], (HID, 128))
    for p in range(GROUP // 2):
        to_pack[p] = jnp.concatenate([pick(2 * p, True), pick(2 * p + 1, True)], axis=0)
        to_edge[p] = jnp.concatenate([pick(2 * p, False), pick(2 * p + 1, False)], axis=1)


def taps_kernel(kp, table, out):
    idx = table[lax.axis_index("lat")]

    def group(g, carry):
        for k in range(16):
            c = g * 16 + k
            row = jnp.broadcast_to(kp[pl.ds(c, 1), :], (ROWS, 128))
            taps = jnp.concatenate(
                [
                    jnp.take_along_axis(row, idx[:, :128], axis=1),
                    jnp.take_along_axis(row, idx[:, 128:], axis=1),
                ],
                axis=1,
            )
            high = taps.astype(bf16)
            out[c, 0:ROWS, :] = high
            out[c, ROWS : 2 * ROWS, :] = (taps - high.astype(f32)).astype(bf16)
        return carry

    lax.fori_loop(0, C // 16, group, 0)


def pack_kernel(x_ref, hs, to_pack, right_ref, left_ref):
    total = jnp.zeros((2 * M * NG * ROWS, 256), f32)
    for p in range(GROUP // 2):
        lhs = jnp.concatenate(
            [
                jnp.concatenate(
                    [
                        ref[m, g * GROUP + 2 * p + d]
                        for ref in (x_ref, hs)
                        for m in range(M)
                        for g in range(NG)
                    ],
                    axis=0,
                )
                for d in range(2)
            ],
            axis=1,
        )
        total = total + jnp.dot(lhs, to_pack[p], preferred_element_type=f32)
    packed = total.astype(bf16).reshape(2, M * NG, ROWS, 256)
    for k in range(2):
        right_ref[:, k * ROWS : (k + 1) * ROWS, :] = packed[k, :, :, :128]
        left_ref[:, k * ROWS : (k + 1) * ROWS, :] = packed[k, :, :, 128:]


def spread_edges(from_left, from_right, to_edge, edge):
    lhs = jnp.concatenate(
        [
            jnp.concatenate(
                [ref[q, k * ROWS : (k + 1) * ROWS, :] for k in range(2) for q in range(M * NG)],
                axis=0,
            )
            for ref in (from_left, from_right)
        ],
        axis=1,
    )
    for p in range(GROUP // 2):
        tiles = jnp.dot(lhs, to_edge[p], preferred_element_type=f32).astype(bf16)
        for d in range(2):
            part = tiles[:, d * 128 : (d + 1) * 128].reshape(2, M * NG, ROWS, 128)
            for k in range(2):
                for q in range(M * NG):
                    edge[k, q // NG, (q % NG) * GROUP + 2 * p + d] = part[k, q]


def shifted(x_ref, hs, edge, c, lane, zero):
    cols = []
    for m in range(M):
        pairs = ((hs[m, c], edge[1, m, c]), (x_ref[m, c], edge[0, m, c]))
        parts = []
        for s in range(-3, 4):
            for v, e in pairs:
                if s > 0:
                    v = pltpu.roll(jnp.where(lane < s, e, v), 128 - s, 1)
                elif s < 0:
                    v = pltpu.roll(jnp.where(lane >= 128 + s, e, v), -s, 1)
                parts.append(v)
        parts += [zero, zero]
        cols.append(jnp.concatenate(parts, axis=0))
    return jnp.concatenate(cols, axis=1)


def block_kernel(
    x_ref, hs, fl, fr, cot_ref, t_ref, diag_ref, to_edge,
    win_t, win, wout, wout_t, vecs, bin_ref,
    out_ref, g_ref, grad_ref,
    edge, cv, ct, pre, ga, act, gp, gwo, gwi,
):
    lane = lax.broadcasted_iota(jnp.int32, (ROWS, 128), 1)
    zero = jnp.zeros((ROWS, 128), bf16)
    lat = lax.axis_index("lat")
    cbias, gain, nbias, bout, scale = (vecs.at[k] for k in range(5))
    spread_edges(fl, fr, to_edge, edge)

    def conv_group(g, carry):
        for cc in range(GROUP):
            c = g * GROUP + cc
            col = shifted(x_ref, hs, edge, c, lane, zero)
            r = jnp.dot(t_ref[c], col, preferred_element_type=f32)
            r = r[:ROWS] + r[ROWS:]
            for m in range(M):
                cv[m, :, c, :] = r[:, m * 128 : (m + 1) * 128]
                ct[m, :, c, :] = cot_ref[m, c].astype(f32)
        return carry

    lax.fori_loop(0, NG, conv_group, 0)
    gwo[...] = jnp.zeros_like(gwo)
    gwi[...] = jnp.zeros_like(gwi)

    def wide(ref):
        return jnp.concatenate([ref[...], ref[...]], axis=1)

    def mlp_chunk(q, carry):
        m = q // 8
        i = (q % 8) * 2
        conv = jnp.concatenate([cv[m, i], cv[m, i + 1]], axis=1) + wide(cbias)
        centred = conv - jnp.mean(conv, axis=0, keepdims=True)
        inv_std = lax.rsqrt(jnp.mean(centred * centred, axis=0, keepdims=True) + eps_norm)
        x_hat = centred * inv_std
        normed = (x_hat * wide(gain) + wide(nbias)).astype(bf16)
        g_mlp = (wide(scale) * jnp.concatenate([ct[m, i], ct[m, i + 1]], axis=1)).astype(bf16)
        pre[...] = jnp.dot(win_t[...], normed, preferred_element_type=f32)
        ga[...] = jnp.dot(wout[...], g_mlp, preferred_element_type=f32)
        for b in range(HID // 32):
            s = pl.ds(b * 32, 32)
            bias = bin_ref[s, :]
            p = pre[s, :] + jnp.concatenate([bias, bias], axis=1)
            phi = 0.5 * (1.0 + lax.erf(p * inv_root_two))
            act[s, :] = (p * phi).astype(bf16)
            slope = phi + p * jnp.exp(-0.5 * p * p) * inv_root_tau
            gp[s, :] = (ga[s, :] * slope).astype(bf16)
        mlp = jnp.dot(wout_t[...], act[...], preferred_element_type=f32)
        res = wide(scale) * (mlp + wide(bout))
        ct[m, i] = res[:, :128]
        ct[m, i + 1] = res[:, 128:]
        g_hat = jnp.dot(win[...], gp[...], preferred_element_type=f32) * wide(gain)
        m1 = jnp.mean(g_hat, axis=0, keepdims=True)
        m2 = jnp.mean(g_hat * x_hat, axis=0, keepdims=True)
        g_conv = inv_std * (g_hat - m1 - x_hat * m2)
        cv[m, i] = g_conv[:, :128]
        cv[m, i + 1] = g_conv[:, 128:]
        across = (((1,), (1,)), ((), ()))
        gwo[...] += lax.dot_general(act[...], g_mlp, across, preferred_element_type=f32)
        gwi[...] += lax.dot_general(gp[...], normed, across, preferred_element_type=f32)
        return carry

    lax.fori_loop(0, M * ROWS // 2, mlp_chunk, 0)
    grad_ref[0:768, :] = gwo[:, 0:128].astype(bf16)
    grad_ref[768:1536, :] = gwi[:, 0:128].astype(bf16)
    grad_ref[1536:2304, :] = jnp.concatenate([gwo[:, 128:192], gwi[:, 128:192]], axis=1).astype(bf16)

    def tap_group(g, carry):
        rows = []
        for cc in range(GROUP):
            c = g * GROUP + cc
            col = shifted(x_ref, hs, edge, c, lane, zero)
            tiles = []
            for m in range(M):
                tile = cv[m, :, c, :].astype(bf16)
                g_ref[m, c] = tile
                tiles.append(tile)
                out_ref[m, c] = (x_ref[m, c].astype(f32) + ct[m, :, c, :]).astype(bf16)
            r = lax.dot_general(
                jnp.concatenate(tiles, axis=1), col, (((1,), (1,)), ((), ())),
                preferred_element_type=f32,
            )
            d0 = jnp.take_along_axis(r[:, :128], diag_ref[lat, 0], axis=1)
            d1 = jnp.take_along_axis(r[:, 128:], diag_ref[lat, 1], axis=1)
            d = jnp.where(lane < 32, d0, d1)
            rows.append(jnp.sum(d, axis=0, keepdims=True))
        start = pl.multiple_of(2304 + g * GROUP, GROUP)
        grad_ref[pl.ds(start, GROUP), :] = jnp.concatenate(rows, axis=0).astype(bf16)
        return carry

    lax.fori_loop(0, NG, tap_group, 0)
    grad_ref[2496:FLAT, :] = jnp.zeros((FLAT - 2496, 128), bf16)


def back_kernel(
    g_ref, hs, fl, fr, cot_ref, t_ref, to_edge, out_ref, edge
):
    lane = lax.broadcasted_iota(jnp.int32, (ROWS, 128), 1)
    zero = jnp.zeros((ROWS, 128), bf16)
    spread_edges(fl, fr, to_edge, edge)

    def group(g, carry):
        for cc in range(GROUP):
            c = g * GROUP + cc
            col = shifted(g_ref, hs, edge, c, lane, zero)
            r = jnp.dot(t_ref[c], col, preferred_element_type=f32)
            r = r[:ROWS] + r[ROWS:]
            for m in range(M):
                back = r[:, m * 128 : (m + 1) * 128]
                out_ref[m, c] = (cot_ref[m, c].astype(f32) + back).astype(bf16)
        return carry

    lax.fori_loop(0, NG, group, 0)


EDGE = pltpu.VMEM((2, M, C, ROWS, LON), bf16)


def routes():
    def flat(lat, lon):
        return lat * N_LON + lon % N_LON

    first = {0: (1, 0), 1: (0, 0), 2: (3, 0), 3: (2, 0)}
    second = {0: (0, 16), 1: (2, 0), 2: (1, 0), 3: (3, 16)}
    return [
        [
            (flat(lat, lon), flat(step[lat][0], lon + step[lat][1]))
            for lat in range(N_LAT)
            for lon in range(N_LON)
        ]
        for step in (first, second)
    ]


def exchange_rows(x, even):
    p1, p2 = routes()
    low = x[:, :, :4]
    high = x[:, :, 12:]
    r1 = lax.ppermute(jnp.where(even, high, low), ("lat", "lon"), p1)
    r2 = lax.ppermute(jnp.where(even, low, high), ("lat", "lon"), p2)
    return jnp.concatenate([r1, r2, jnp.zeros((M, C, 8, LON), bf16)], axis=2)


def pack(x, hs, to_pack):
    packed = jax.ShapeDtypeStruct((M * NG, 2 * ROWS, LON), bf16)
    return pl.pallas_call(
        pack_kernel, out_shape=(packed, packed), compiler_params=PARAMS, name="pack"
    )(x, hs, to_pack)


def exchange_cols(right, left):
    forward = [(i, (i + 1) % N_LON) for i in range(N_LON)]
    backward = [(t, s) for s, t in forward]
    return lax.ppermute(right, "lon", forward), lax.ppermute(left, "lon", backward)


def tap_matrix(taps, table):
    return pl.pallas_call(
        taps_kernel,
        out_shape=jax.ShapeDtypeStruct((C, 2 * ROWS, 256), bf16),
        compiler_params=PARAMS,
        name="taps",
    )(taps, table)


def shards(
    inputs, cotangent, kernel, conv_bias, norm_gain, norm_bias,
    w_in, bias_in, w_out, bias_out, layer_scale,
):
    both = ("lat", "lon")
    even = lax.axis_index("lat") % 2 == 0
    tile = jax.ShapeDtypeStruct((M, C, ROWS, LON), bf16)
    taps = jnp.pad(jnp.swapaxes(kernel, 1, 2), ((0, 0), (0, 0), (0, 1)))
    taps = jnp.pad(taps.reshape(C, 56), ((0, 0), (0, 72)))
    rows = (conv_bias, norm_gain, norm_bias, bias_out, layer_scale)
    onehot = jax.ShapeDtypeStruct((GROUP // 2, 256, 256), bf16)
    vecs, bias_wide, to_pack, to_edge = pl.pallas_call(
        maps_kernel,
        out_shape=(
            jax.ShapeDtypeStruct((5, C, 128), f32),
            jax.ShapeDtypeStruct((HID, 128), f32), onehot, onehot,
        ),
        compiler_params=PARAMS,
        name="maps",
    )(jnp.stack(rows + rows[:3]), jnp.broadcast_to(bias_in[None], (8, HID)))
    hs = exchange_rows(inputs, even)
    right, left = pack(inputs, hs, to_pack)
    taps, right, left = lax.optimization_barrier((taps, right, left))
    from_left, from_right = exchange_cols(right, left)
    t_fwd = tap_matrix(taps, FWD_TABLE)
    output, g_round, grads = pl.pallas_call(
        block_kernel,
        out_shape=(tile, tile, jax.ShapeDtypeStruct((FLAT, 128), bf16)),
        scratch_shapes=[
            EDGE,
            pltpu.VMEM((M, ROWS, C, LON), f32),
            pltpu.VMEM((M, ROWS, C, LON), f32),
            pltpu.VMEM((HID, CELLS), f32),
            pltpu.VMEM((HID, CELLS), f32),
            pltpu.VMEM((HID, CELLS), bf16),
            pltpu.VMEM((HID, CELLS), bf16),
            pltpu.VMEM((HID, C), f32),
            pltpu.VMEM((HID, C), f32),
        ],
        compiler_params=PARAMS,
        name="block",
    )(
        inputs, hs, from_left, from_right, cotangent, t_fwd, DIAG_TABLE, to_edge,
        w_in.T, w_in, w_out, w_out.T, vecs, bias_wide,
    )
    parts = lax.all_to_all(grads.reshape(128, CHUNK_ROWS, 128), both, 0, 0, tiled=True)
    g_halo = exchange_rows(g_round, even)
    g_right, g_left = pack(g_round, g_halo, to_pack)
    taps, grads = lax.optimization_barrier((taps, grads))
    t_spr = tap_matrix(taps, SPR_TABLE)
    factor = 1.0 / math.sqrt(M * ROWS * N_LAT * LON * N_LON)
    mine = (jnp.sum(parts.astype(f32), axis=0) * factor).astype(bf16)
    mine, g_right, g_left, t_spr = lax.optimization_barrier((mine, g_right, g_left, t_spr))
    grad_input = pl.pallas_call(
        back_kernel, out_shape=tile, scratch_shapes=[EDGE], compiler_params=PARAMS, name="back"
    )(g_round, g_halo, *exchange_cols(g_right, g_left), cotangent, t_spr, to_edge)
    every = lax.all_to_all(
        jnp.broadcast_to(mine[None], (128, CHUNK_ROWS, 128)), both, 0, 0, tiled=True
    ).reshape(FLAT, 128)
    every = every.astype(f32)
    grad_out = jnp.concatenate([every[0:768], every[1536:2304, :64]], axis=1)
    grad_in = jnp.concatenate([every[768:1536], every[1536:2304, 64:]], axis=1).T
    taps = every[2304:2496, :56].reshape(C, TAPS, 8)[:, :, :TAPS]
    grad_kernel = jnp.swapaxes(taps, 1, 2)
    return output, grad_input, grad_kernel, grad_in, grad_out


def solution(mesh):
    placed = (P(None, None, "lat", "lon"),) * 2 + (P(),) * 9
    return jax.shard_map(
        shards,
        mesh=mesh,
        in_specs=placed,
        out_specs=(P(None, None, "lat", "lon"),) * 2 + (P(),) * 3,
        check_vma=False,
    )
```

```python
import math

import jax
import jax.numpy as jnp
import numpy as np
from jax import lax
from jax.experimental import pallas as pl
from jax.experimental.pallas import tpu as pltpu
from jax.sharding import PartitionSpec as P

eps_norm = 1e-06
inv_root_two = 0.7071067811865476
inv_root_tau = 0.3989422804014327
f32 = jnp.float32
bf16 = jnp.bfloat16

M, C, HID, ROWS, LON = 2, 192, 768, 16, 128
GROUP = 32
NG = C // GROUP
TAPS = 7
OWN_K = TAPS * 16
DEPTH = OWN_K + 64
N_LAT, N_LON = 4, 32
PITCH = C + 8
CELLS = 256
CHUNK_ROWS = 24
FLAT = 128 * CHUNK_ROWS
PARAMS = pltpu.CompilerParams(vmem_limit_bytes=60 * 2**20)


def halo_row(lat, pos):
    half, k = divmod(pos, 4)
    if lat == 0:
        return 16 + k if half == 0 else -1 - k
    if lat == 1:
        return k - 4 if half == 0 else 16 + k
    if lat == 2:
        return 16 + k if half == 0 else k - 4
    return k - 4 if half == 0 else 19 - k


def tap_tables():
    fwd = np.full((N_LAT, ROWS, 256), 127, np.int32)
    spr = np.full((N_LAT, ROWS, 256), 127, np.int32)
    diag = np.zeros((N_LAT, 3, ROWS, 128), np.int32)
    for lat in range(N_LAT):
        for i in range(ROWS):
            for t in range(TAPS):
                for pos in range(24):
                    k = pos % 4
                    row = pos - 8 if pos >= 8 else halo_row(lat, pos)
                    a_fwd = row - i + 3
                    a_spr = i - row + 3
                    if lat == 0 and 4 <= pos < 8:
                        a_spr = 2 - i - k
                    if lat == 3 and 4 <= pos < 8:
                        a_spr = 22 - i - k
                    if pos >= 8:
                        source = t * 16 + pos - 8
                    else:
                        source = OWN_K + t * 8 + pos
                    if 0 <= a_fwd < TAPS:
                        fwd[lat, i, source] = t * 8 + a_fwd
                        diag[lat, source // 128, i, t * 8 + a_fwd] = source % 128
                        diag[lat, 2, i, t * 8 + a_fwd] = source // 128
                    if 0 <= a_spr < TAPS:
                        spr[lat, i, source] = (6 - t) * 8 + a_spr
    return fwd, spr, diag


FWD_TABLE, SPR_TABLE, DIAG_TABLE = tap_tables()


def pick(cc, transposed):
    shape = (128, 256) if transposed else (256, 128)
    packed = lax.broadcasted_iota(jnp.int32, shape, 1 if transposed else 0)
    lane = lax.broadcasted_iota(jnp.int32, shape, 0 if transposed else 1)
    k = packed % 128 - 4 * cc
    hit = (k >= 0) & (k < 3) & (lane == k + jnp.where(packed < 128, 125, 0))
    return jnp.where(hit, 1.0, 0.0).astype(bf16)


def own_pack_kernel(x_ref, right_ref, left_ref):
    total = jnp.zeros((M * NG * ROWS, 256), f32)
    for cc in range(0, GROUP, 2):
        total = total + edge_product(x_ref, cc)
    packed = total.astype(bf16).reshape(M * NG, ROWS, 256)
    right_ref[...] = packed[:, :, :128]
    left_ref[...] = packed[:, :, 128:]


def edge_product(x_ref, cc):
    lhs = jnp.concatenate(
        [
            jnp.concatenate(
                [x_ref[m, g * GROUP + cc + d] for m in range(M) for g in range(NG)], axis=0
            )
            for d in range(2)
        ],
        axis=1,
    )
    rhs = jnp.concatenate([pick(cc, True), pick(cc + 1, True)], axis=0)
    return jnp.dot(lhs, rhs, preferred_element_type=f32)


def halo_pack_kernel(r1, r2, own_right, own_left, hs, right_ref, left_ref):
    def channel(c, carry):
        for m in range(M):
            hs[m, c] = jnp.concatenate([r1[m, c], r2[m, c], r1[m, c], r2[m, c]], axis=0)
        return carry

    lax.fori_loop(0, C, channel, 0, unroll=8)
    total = jnp.zeros((M * NG * ROWS, 256), f32)
    for cc in range(0, GROUP, 2):
        total = total + edge_product(hs, cc)
    packed = total.astype(bf16).reshape(M * NG, ROWS, 256)
    right_ref[:, 0:ROWS, :] = own_right[...]
    left_ref[:, 0:ROWS, :] = own_left[...]
    right_ref[:, ROWS : 2 * ROWS, :] = packed[:, :, :128]
    left_ref[:, ROWS : 2 * ROWS, :] = packed[:, :, 128:]


def spread_edges(from_left, from_right, edge):
    lhs = jnp.concatenate(
        [
            jnp.concatenate(
                [ref[q, k * ROWS : (k + 1) * ROWS, :] for k in range(2) for q in range(M * NG)],
                axis=0,
            )
            for ref in (from_left, from_right)
        ],
        axis=1,
    )
    for cc in range(0, GROUP, 2):
        rhs = jnp.concatenate([pick(cc, False), pick(cc + 1, False)], axis=1)
        tiles = jnp.dot(lhs, rhs, preferred_element_type=f32).astype(bf16)
        for d in range(2):
            part = tiles[:, d * 128 : (d + 1) * 128].reshape(2, M * NG, ROWS, 128)
            for k in range(2):
                for q in range(M * NG):
                    edge[k, q // NG, (q % NG) * GROUP + cc + d] = part[k, q]


def tap_tile(kp, idx, c):
    row = jnp.broadcast_to(kp[pl.ds(c, 1), :], (ROWS, 128))
    taps = jnp.concatenate(
        [
            jnp.take_along_axis(row, idx[:, :128], axis=1),
            jnp.take_along_axis(row, idx[:, 128:], axis=1),
        ],
        axis=1,
    )
    high = taps.astype(bf16)
    both = jnp.concatenate([high, (taps - high.astype(f32)).astype(bf16)], axis=0)
    return both[:, :DEPTH]


def group_copy(src, dst, sem, g):
    part = pl.ds(pl.multiple_of(g * GROUP, GROUP), GROUP)
    return pltpu.make_async_copy(src.at[:, part], dst.at[:, part], sem.at[g])


def shifted(x_ref, hs, edge, c, lane, top):
    cols = []
    for m in range(M):
        parts = []
        for v, e in ((x_ref[m, c], edge[0, m, c]), (hs[m, c], edge[1, m, c])):
            for s in range(-3, 4):
                if s > 0:
                    w = pltpu.roll(jnp.where(lane < s, e, v), 128 - s, 1)
                elif s < 0:
                    w = pltpu.roll(jnp.where(lane >= 128 + s, e, v), -s, 1)
                else:
                    w = v
                parts.append(w)
        halo = parts[TAPS:]
        pairs = [jnp.where(top, halo[p], halo[p + 1]) for p in (0, 2, 4)]
        cols.append(jnp.concatenate(parts[:TAPS] + pairs + [halo[6]], axis=0))
    return jnp.concatenate(cols, axis=1)


def block_kernel(
    x_hbm, h_hbm, cot_hbm, win_hbm, wout_hbm, fl, fr, kp, table, vec, bias,
    out_hbm, g_hbm, g1_ref, g2_ref, grad_ref,
    x_ref, hs, cot_ref, g_ref, win, wout, win_t, wout_t, vecs, bin_ref,
    edge, cv, ct, gv, rv, pre, ga, act, gp, nrm, gm, xh, inv, gwo, gwi,
    x_sem, h_sem, cot_sem, w_sem, out_sem, g_sem,
):
    lat = lax.axis_index("lat")
    streams = ((x_hbm, x_ref, x_sem), (h_hbm, hs, h_sem), (cot_hbm, cot_ref, cot_sem))
    for g in range(NG):
        for src, dst, sem in streams:
            group_copy(src, dst, sem, g).start()
    win_copy = pltpu.make_async_copy(win_hbm, win, w_sem.at[0])
    wout_copy = pltpu.make_async_copy(wout_hbm, wout_t, w_sem.at[1])
    win_copy.start()
    wout_copy.start()
    lane = lax.broadcasted_iota(jnp.int32, (ROWS, 128), 1)
    top = lax.broadcasted_iota(jnp.int32, (ROWS, 128), 0) < 8
    columns = jnp.transpose(vec[...])
    for k in range(5):
        vecs[k] = jnp.broadcast_to(columns[:, k : k + 1], (C, 128))
    cbias, gain, nbias, bout, scale = (vecs.at[k] for k in range(5))
    columns = jnp.transpose(bias[...])
    bin_ref[...] = jnp.broadcast_to(columns[:, 0:1], (HID, 128))
    spread_edges(fl, fr, edge)
    idx = table[lat]

    def conv_group(g, carry):
        for src, dst, sem in streams:
            group_copy(src, dst, sem, g).wait()
        for cc in range(GROUP):
            c = g * GROUP + cc
            col = shifted(x_ref, hs, edge, c, lane, top)
            r = jnp.dot(tap_tile(kp, idx, c), col, preferred_element_type=f32)
            r = r[:ROWS] + r[ROWS:]
            for m in range(M):
                cv[m, :, c, :] = r[:, m * 128 : (m + 1) * 128]
                ct[m, :, c, :] = cot_ref[m, c].astype(f32)
        return carry

    lax.fori_loop(0, NG, conv_group, 0)
    win_copy.wait()
    wout_copy.wait()
    win_t[...] = jnp.transpose(win[...])
    wout[...] = jnp.transpose(wout_t[...])
    gwo[...] = jnp.zeros_like(gwo)
    gwi[...] = jnp.zeros_like(gwi)

    def wide(ref):
        return jnp.concatenate([ref[...], ref[...]], axis=1)

    def rows_of(q):
        return q // 8, (q % 8) * 2

    def norm_steps(q, b):
        m, i = rows_of(q)
        conv = jnp.concatenate([cv[m, i, 0:C, :], cv[m, i + 1, 0:C, :]], axis=1) + wide(cbias)
        centred = conv - jnp.mean(conv, axis=0, keepdims=True)
        inv_std = lax.rsqrt(jnp.mean(centred * centred, axis=0, keepdims=True) + eps_norm)
        x_hat = centred * inv_std
        xh[b] = x_hat
        inv[b] = jnp.broadcast_to(inv_std, (8, CELLS))
        nrm[b] = (x_hat * wide(gain) + wide(nbias)).astype(bf16)
        gm[b] = (wide(scale) * jnp.concatenate([ct[m, i, 0:C, :], ct[m, i + 1, 0:C, :]], axis=1)).astype(bf16)
        yield
        pre[b] = jnp.dot(win_t[...], nrm[b], preferred_element_type=f32)
        yield
        ga[b] = jnp.dot(wout[...], gm[b], preferred_element_type=f32)
        yield

    def gelu_steps(b):
        for blk in range(HID // 32):
            s = pl.ds(blk * 32, 32)
            bias = bin_ref[s, :]
            p = pre[b, s, :] + jnp.concatenate([bias, bias], axis=1)
            phi = 0.5 * (1.0 + lax.erf(p * inv_root_two))
            act[b, s, :] = (p * phi).astype(bf16)
            slope = phi + p * jnp.exp(-0.5 * p * p) * inv_root_tau
            gp[b, s, :] = (ga[b, s, :] * slope).astype(bf16)
            yield

    def out_steps(q, b):
        m, i = rows_of(q)
        across = (((1,), (1,)), ((), ()))
        mlp = jnp.dot(wout_t[...], act[b], preferred_element_type=f32)
        res = wide(scale) * (mlp + wide(bout))
        rv[m, i, 0:C, :] = res[:, :128]
        rv[m, i + 1, 0:C, :] = res[:, 128:]
        yield
        g_hat = jnp.dot(win[...], gp[b], preferred_element_type=f32) * wide(gain)
        yield
        x_hat = xh[b]
        m1 = jnp.mean(g_hat, axis=0, keepdims=True)
        m2 = jnp.mean(g_hat * x_hat, axis=0, keepdims=True)
        g_conv = inv[b, 0:1, :] * (g_hat - m1 - x_hat * m2)
        gv[m, i, 0:C, :] = g_conv[:, :128]
        gv[m, i + 1, 0:C, :] = g_conv[:, 128:]
        yield
        gwo[...] += lax.dot_general(act[b], gm[b], across, preferred_element_type=f32)
        yield
        gwi[...] += lax.dot_general(gp[b], nrm[b], across, preferred_element_type=f32)
        yield

    def weave(gelu, others):
        share = HID // 32 // sum(n for _, n in others)
        for it, n in others:
            for _ in range(n):
                next(it, None)
                for _ in range(share):
                    next(gelu, None)
        for _ in gelu:
            pass
        for it, _ in others:
            for _ in it:
                pass

    for _ in norm_steps(0, 0):
        pass
    weave(gelu_steps(0), [(norm_steps(1, 1), 3)])

    def mlp_pair(j, carry):
        q = 2 * j + 1
        weave(gelu_steps(1), [(out_steps(q - 1, 0), 5), (norm_steps(q + 1, 0), 3)])
        weave(gelu_steps(0), [(out_steps(q, 1), 5), (norm_steps(q + 2, 1), 3)])
        return carry

    lax.fori_loop(0, 7, mlp_pair, 0)
    weave(gelu_steps(1), [(out_steps(14, 0), 5)])
    for _ in out_steps(15, 1):
        pass
    grad_ref[0:768, :] = gwo[:, 0:128].astype(bf16)
    grad_ref[768:1536, :] = gwi[:, 0:128].astype(bf16)
    grad_ref[1536:2304, :] = jnp.concatenate([gwo[:, 128:192], gwi[:, 128:192]], axis=1).astype(bf16)

    grad_ref[2304:FLAT, :] = jnp.zeros((FLAT - 2304, 128), bf16)
    even = lat % 2 == 0

    def out_group(g, carry):
        for cc in range(GROUP):
            c = g * GROUP + cc
            for m in range(M):
                tile = gv[m, :, c, :].astype(bf16)
                g_ref[m, c] = tile
                cot_ref[m, c] = (x_ref[m, c].astype(f32) + rv[m, :, c, :]).astype(bf16)
                low, high = tile[0:4], tile[12:16]
                g1_ref[m, c] = jnp.where(even, high, low)
                g2_ref[m, c] = jnp.where(even, low, high)
        group_copy(cot_ref, out_hbm, out_sem, g).start()
        group_copy(g_ref, g_hbm, g_sem, g).start()
        return carry

    lax.fori_loop(0, NG, out_group, 0)
    for g in range(NG):
        group_copy(cot_ref, out_hbm, out_sem, g).wait()
        group_copy(g_ref, g_hbm, g_sem, g).wait()


def tap_kernel(
    x_hbm, h_hbm, g_hbm, grads_in, fl, fr, diag_ref, grads_hbm,
    x_ref, hs, g_ref, edge, sums, x_sem, h_sem, g_sem, sum_sem,
):
    streams = ((x_hbm, x_ref, x_sem), (h_hbm, hs, h_sem), (g_hbm, g_ref, g_sem))
    for g in range(NG):
        for src, dst, sem in streams:
            group_copy(src, dst, sem, g).start()
    lat = lax.axis_index("lat")
    lane = lax.broadcasted_iota(jnp.int32, (ROWS, 128), 1)
    top = lax.broadcasted_iota(jnp.int32, (ROWS, 128), 0) < 8
    second = diag_ref[lat, 2] == 1
    blank = jnp.zeros((ROWS, 256 - DEPTH), f32)
    spread_edges(fl, fr, edge)

    def tap_group(g, carry):
        for src, dst, sem in streams:
            group_copy(src, dst, sem, g).wait()
        rows = []
        for cc in range(GROUP):
            c = g * GROUP + cc
            col = shifted(x_ref, hs, edge, c, lane, top)
            r = lax.dot_general(
                jnp.concatenate([g_ref[m, c] for m in range(M)], axis=1), col,
                (((1,), (1,)), ((), ())), preferred_element_type=f32,
            )
            d0 = jnp.take_along_axis(r[:, :128], diag_ref[lat, 0], axis=1)
            rest = jnp.concatenate([r[:, 128:], blank], axis=1)
            d1 = jnp.take_along_axis(rest, diag_ref[lat, 1], axis=1)
            d = jnp.where(second, d1, d0)
            rows.append(jnp.sum(d, axis=0, keepdims=True))
        start = pl.multiple_of(g * GROUP, GROUP)
        sums[pl.ds(start, GROUP), :] = jnp.concatenate(rows, axis=0).astype(bf16)
        return carry

    lax.fori_loop(0, NG, tap_group, 0)
    copy = pltpu.make_async_copy(sums, grads_hbm.at[pl.ds(2304, C)], sum_sem.at[0])
    copy.start()
    copy.wait()


def back_kernel(
    x_hbm, h_hbm, cot_hbm, fl, fr, kp, table, out_hbm,
    g_ref, hs, cot_ref, edge, x_sem, h_sem, cot_sem, out_sem,
):
    streams = ((x_hbm, g_ref, x_sem), (h_hbm, hs, h_sem), (cot_hbm, cot_ref, cot_sem))
    for g in range(NG):
        for src, dst, sem in streams:
            group_copy(src, dst, sem, g).start()
    lane = lax.broadcasted_iota(jnp.int32, (ROWS, 128), 1)
    top = lax.broadcasted_iota(jnp.int32, (ROWS, 128), 0) < 8
    spread_edges(fl, fr, edge)
    idx = table[lax.axis_index("lat")]

    def group(g, carry):
        for src, dst, sem in streams:
            group_copy(src, dst, sem, g).wait()
        for cc in range(GROUP):
            c = g * GROUP + cc
            col = shifted(g_ref, hs, edge, c, lane, top)
            r = jnp.dot(tap_tile(kp, idx, c), col, preferred_element_type=f32)
            r = r[:ROWS] + r[ROWS:]
            for m in range(M):
                back = r[:, m * 128 : (m + 1) * 128]
                cot_ref[m, c] = (cot_ref[m, c].astype(f32) + back).astype(bf16)
        group_copy(cot_ref, out_hbm, out_sem, g).start()
        return carry

    lax.fori_loop(0, NG, group, 0)
    for g in range(NG):
        group_copy(cot_ref, out_hbm, out_sem, g).wait()


EDGE = pltpu.VMEM((2, M, C, ROWS, LON), bf16)
TILES = pltpu.VMEM((M, C, ROWS, LON), bf16)
SEMS = pltpu.SemaphoreType.DMA((NG,))
ANY = pl.BlockSpec(memory_space=pl.ANY)
VMEM = pl.BlockSpec(memory_space=pltpu.VMEM)
BLOCK_SCRATCH = [
    TILES,
    TILES,
    TILES,
    TILES,
    pltpu.VMEM((C, HID), bf16),
    pltpu.VMEM((HID, C), bf16),
    pltpu.VMEM((HID, C), bf16),
    pltpu.VMEM((C, HID), bf16),
    pltpu.VMEM((5, C, 128), f32),
    pltpu.VMEM((HID, 128), f32),
    EDGE,
    pltpu.VMEM((M, ROWS, PITCH, LON), f32),
    pltpu.VMEM((M, ROWS, PITCH, LON), f32),
    pltpu.VMEM((M, ROWS, PITCH, LON), f32),
    pltpu.VMEM((M, ROWS, PITCH, LON), f32),
    pltpu.VMEM((2, HID, CELLS), f32),
    pltpu.VMEM((2, HID, CELLS), f32),
    pltpu.VMEM((2, HID, CELLS), bf16),
    pltpu.VMEM((2, HID, CELLS), bf16),
    pltpu.VMEM((2, C, CELLS), bf16),
    pltpu.VMEM((2, C, CELLS), bf16),
    pltpu.VMEM((2, C, CELLS), f32),
    pltpu.VMEM((2, 8, CELLS), f32),
    pltpu.VMEM((HID, C), f32),
    pltpu.VMEM((HID, C), f32),
    SEMS,
    SEMS,
    SEMS,
    pltpu.SemaphoreType.DMA((2,)),
    SEMS,
    SEMS,
]


def routes():
    def flat(lat, lon):
        return lat * N_LON + lon % N_LON

    first = {0: (1, 0), 1: (0, 0), 2: (3, 0), 3: (2, 0)}
    second = {0: (0, 16), 1: (2, 0), 2: (1, 0), 3: (3, 16)}
    return [
        [
            (flat(lat, lon), flat(step[lat][0], lon + step[lat][1]))
            for lat in range(N_LAT)
            for lon in range(N_LON)
        ]
        for step in (first, second)
    ]


def exchange_rows(first, second):
    p1, p2 = routes()
    both = ("lat", "lon")
    return lax.ppermute(first, both, p1), lax.ppermute(second, both, p2)


def own_pack(x):
    own = jax.ShapeDtypeStruct((M * NG, ROWS, LON), bf16)
    return pl.pallas_call(
        own_pack_kernel, out_shape=(own, own), compiler_params=PARAMS, name="own_pack"
    )(x)


def halo_pack(r1, r2, right, left):
    packed = jax.ShapeDtypeStruct((M * NG, 2 * ROWS, LON), bf16)
    return pl.pallas_call(
        halo_pack_kernel,
        out_shape=(jax.ShapeDtypeStruct((M, C, ROWS, LON), bf16), packed, packed),
        compiler_params=PARAMS,
        name="halo_pack",
    )(r1, r2, right, left)


def tap_sums(x, hs, g_round, from_left, from_right, grads):
    return pl.pallas_call(
        tap_kernel,
        out_shape=jax.ShapeDtypeStruct((FLAT, 128), bf16),
        in_specs=[ANY] * 4 + [VMEM] * 3,
        out_specs=ANY,
        scratch_shapes=[
            TILES, TILES, TILES, EDGE, pltpu.VMEM((C, 128), bf16),
            SEMS, SEMS, SEMS, pltpu.SemaphoreType.DMA((1,)),
        ],
        input_output_aliases={3: 0},
        compiler_params=PARAMS,
        name="tap_sums",
    )(x, hs, g_round, grads, from_left, from_right, DIAG_TABLE)


def exchange_cols(right, left):
    forward = [(i, (i + 1) % N_LON) for i in range(N_LON)]
    backward = [(t, s) for s, t in forward]
    return lax.ppermute(right, "lon", forward), lax.ppermute(left, "lon", backward)


def shards(
    inputs, cotangent, kernel, conv_bias, norm_gain, norm_bias,
    w_in, bias_in, w_out, bias_out, layer_scale,
):
    both = ("lat", "lon")
    even = lax.axis_index("lat") % 2 == 0
    tile = jax.ShapeDtypeStruct((M, C, ROWS, LON), bf16)
    taps = jnp.pad(jnp.swapaxes(kernel, 1, 2), ((0, 0), (0, 0), (0, 1)))
    taps = jnp.pad(taps.reshape(C, 56), ((0, 0), (0, 72)))
    rows = (conv_bias, norm_gain, norm_bias, bias_out, layer_scale)
    low, high = inputs[:, :, :4], inputs[:, :, 12:]
    r1, r2 = exchange_rows(jnp.where(even, high, low), jnp.where(even, low, high))
    vec = jnp.stack(rows + rows[:3])
    bias = jnp.broadcast_to(bias_in[None], (8, HID))
    r1, r2, own, taps, vec, bias = lax.optimization_barrier(
        (r1, r2, own_pack(inputs), taps, vec, bias)
    )
    hs, right, left = halo_pack(r1, r2, *own)
    x_cols = exchange_cols(right, left)
    edge_rows = jax.ShapeDtypeStruct((M, C, 4, LON), bf16)
    output, g_round, g1, g2, grads = pl.pallas_call(
        block_kernel,
        out_shape=(tile, tile, edge_rows, edge_rows, jax.ShapeDtypeStruct((FLAT, 128), bf16)),
        in_specs=[ANY] * 5 + [VMEM] * 6,
        out_specs=(ANY, ANY, VMEM, VMEM, VMEM),
        scratch_shapes=BLOCK_SCRATCH,
        compiler_params=PARAMS,
        name="block",
    )(
        inputs, hs, cotangent, w_in, w_out.T, *x_cols, taps, FWD_TABLE, vec, bias,
    )
    g1, g2, own, grads = lax.optimization_barrier(
        (
            *exchange_rows(g1, g2),
            own_pack(g_round),
            tap_sums(inputs, hs, g_round, *x_cols, grads),
        )
    )
    parts = lax.all_to_all(grads.reshape(128, CHUNK_ROWS, 128), both, 0, 0, tiled=True)
    g_halo, g_right, g_left = halo_pack(g1, g2, *own)
    factor = 1.0 / math.sqrt(M * ROWS * N_LAT * LON * N_LON)
    mine = (jnp.sum(parts.astype(f32), axis=0) * factor).astype(bf16)
    mine, g_cols = lax.optimization_barrier((mine, exchange_cols(g_right, g_left)))
    grad_input = pl.pallas_call(
        back_kernel,
        out_shape=tile,
        in_specs=[ANY] * 3 + [VMEM] * 4,
        out_specs=ANY,
        scratch_shapes=[TILES, TILES, TILES, EDGE, SEMS, SEMS, SEMS, SEMS],
        compiler_params=PARAMS,
        name="back",
    )(g_round, g_halo, cotangent, *g_cols, taps, SPR_TABLE)
    every = lax.all_to_all(
        jnp.broadcast_to(mine[None], (128, CHUNK_ROWS, 128)), both, 0, 0, tiled=True
    ).reshape(FLAT, 128)
    every = every.astype(f32)
    grad_out = jnp.concatenate([every[0:768], every[1536:2304, :64]], axis=1)
    grad_in = jnp.concatenate([every[768:1536], every[1536:2304, 64:]], axis=1).T
    taps = every[2304:2496, :56].reshape(C, TAPS, 8)[:, :, :TAPS]
    grad_kernel = jnp.swapaxes(taps, 1, 2)
    return output, grad_input, grad_kernel, grad_in, grad_out


def solution(mesh):
    placed = (P(None, None, "lat", "lon"),) * 2 + (P(),) * 9
    return jax.shard_map(
        shards,
        mesh=mesh,
        in_specs=placed,
        out_specs=(P(None, None, "lat", "lon"),) * 2 + (P(),) * 3,
        check_vma=False,
    )
```

```python
import math

import jax
import jax.numpy as jnp
import numpy as np
from jax import lax
from jax.experimental import pallas as pl
from jax.experimental.pallas import tpu as pltpu
from jax.sharding import PartitionSpec as P

eps_norm = 1e-06
inv_root_two = 0.7071067811865476
inv_root_tau = 0.3989422804014327
f32 = jnp.float32
bf16 = jnp.bfloat16

M, C, HID, ROWS, LON = 2, 192, 768, 16, 128
GROUP = 32
NG = C // GROUP
TAPS = 7
OWN_K = TAPS * 16
DEPTH = OWN_K + 64
N_LAT, N_LON = 4, 32
PITCH = C + 8
CELLS = 256
CHUNK_ROWS = 24
FLAT = 128 * CHUNK_ROWS
PARAMS = pltpu.CompilerParams(vmem_limit_bytes=60 * 2**20)
SMALL = pltpu.CompilerParams(vmem_limit_bytes=16 * 2**20)


def halo_row(lat, pos):
    half, k = divmod(pos, 4)
    if lat == 0:
        return 16 + k if half == 0 else -1 - k
    if lat == 1:
        return k - 4 if half == 0 else 16 + k
    if lat == 2:
        return 16 + k if half == 0 else k - 4
    return k - 4 if half == 0 else 19 - k


def tap_tables():
    fwd = np.full((N_LAT, ROWS, 256), 127, np.int32)
    spr = np.full((N_LAT, ROWS, 256), 127, np.int32)
    diag = np.zeros((N_LAT, 3, ROWS, 128), np.int32)
    for lat in range(N_LAT):
        for i in range(ROWS):
            for t in range(TAPS):
                for pos in range(24):
                    k = pos % 4
                    row = pos - 8 if pos >= 8 else halo_row(lat, pos)
                    a_fwd = row - i + 3
                    a_spr = i - row + 3
                    if lat == 0 and 4 <= pos < 8:
                        a_spr = 2 - i - k
                    if lat == 3 and 4 <= pos < 8:
                        a_spr = 22 - i - k
                    if pos >= 8:
                        source = t * 16 + pos - 8
                    else:
                        source = OWN_K + t * 8 + pos
                    if 0 <= a_fwd < TAPS:
                        fwd[lat, i, source] = t * 8 + a_fwd
                        diag[lat, source // 128, i, a_fwd * 8 + t] = source % 128
                        diag[lat, 2, i, a_fwd * 8 + t] = source // 128
                    if 0 <= a_spr < TAPS:
                        spr[lat, i, source] = (6 - t) * 8 + a_spr
    return fwd, spr, diag


FWD_TABLE, SPR_TABLE, DIAG_TABLE = tap_tables()


def pick(cc, transposed):
    shape = (128, 256) if transposed else (256, 128)
    packed = lax.broadcasted_iota(jnp.int32, shape, 1 if transposed else 0)
    lane = lax.broadcasted_iota(jnp.int32, shape, 0 if transposed else 1)
    k = packed % 128 - 4 * cc
    hit = (k >= 0) & (k < 3) & (lane == k + jnp.where(packed < 128, 125, 0))
    return jnp.where(hit, 1.0, 0.0).astype(bf16)


def own_pack_kernel(x_ref, right_ref, left_ref):
    total = jnp.zeros((M * NG * ROWS, 256), f32)
    for cc in range(0, GROUP, 2):
        total = total + edge_product(x_ref, cc)
    packed = total.astype(bf16).reshape(M * NG, ROWS, 256)
    right_ref[...] = packed[:, :, :128]
    left_ref[...] = packed[:, :, 128:]


def edge_product(x_ref, cc):
    lhs = jnp.concatenate(
        [
            jnp.concatenate(
                [x_ref[m, g * GROUP + cc + d] for m in range(M) for g in range(NG)], axis=0
            )
            for d in range(2)
        ],
        axis=1,
    )
    rhs = jnp.concatenate([pick(cc, True), pick(cc + 1, True)], axis=0)
    return jnp.dot(lhs, rhs, preferred_element_type=f32)


def halo_pack_kernel(r1, r2, own_right, own_left, hs, right_ref, left_ref):
    def channel(c, carry):
        for m in range(M):
            hs[m, c] = jnp.concatenate([r1[m, c], r2[m, c], r1[m, c], r2[m, c]], axis=0)
        return carry

    lax.fori_loop(0, C, channel, 0, unroll=8)
    total = jnp.zeros((M * NG * ROWS, 256), f32)
    for cc in range(0, GROUP, 2):
        total = total + edge_product(hs, cc)
    packed = total.astype(bf16).reshape(M * NG, ROWS, 256)
    right_ref[:, 0:ROWS, :] = own_right[...]
    left_ref[:, 0:ROWS, :] = own_left[...]
    right_ref[:, ROWS : 2 * ROWS, :] = packed[:, :, :128]
    left_ref[:, ROWS : 2 * ROWS, :] = packed[:, :, 128:]


def spread_edges(from_left, from_right, edge):
    lhs = jnp.concatenate(
        [
            jnp.concatenate(
                [ref[q, k * ROWS : (k + 1) * ROWS, :] for k in range(2) for q in range(M * NG)],
                axis=0,
            )
            for ref in (from_left, from_right)
        ],
        axis=1,
    )
    for cc in range(0, GROUP, 2):
        rhs = jnp.concatenate([pick(cc, False), pick(cc + 1, False)], axis=1)
        tiles = jnp.dot(lhs, rhs, preferred_element_type=f32).astype(bf16)
        for d in range(2):
            part = tiles[:, d * 128 : (d + 1) * 128].reshape(2, M * NG, ROWS, 128)
            for k in range(2):
                for q in range(M * NG):
                    edge[k, q // NG, (q % NG) * GROUP + cc + d] = part[k, q]


def tap_tile(kp, idx, c):
    row = jnp.broadcast_to(kp[pl.ds(c, 1), :], (ROWS, 128))
    taps = jnp.concatenate(
        [
            jnp.take_along_axis(row, idx[:, :128], axis=1),
            jnp.take_along_axis(row, idx[:, 128:], axis=1),
        ],
        axis=1,
    )
    high = taps.astype(bf16)
    both = jnp.concatenate([high, (taps - high.astype(f32)).astype(bf16)], axis=0)
    return both[:, :DEPTH]


def group_copy(src, dst, sem, g):
    part = pl.ds(pl.multiple_of(g * GROUP, GROUP), GROUP)
    return pltpu.make_async_copy(src.at[:, part], dst.at[:, part], sem.at[g])


def shifted(x_ref, hs, edge, c, lane, top):
    cols = []
    for m in range(M):
        parts = []
        for v, e in ((x_ref[m, c], edge[0, m, c]), (hs[m, c], edge[1, m, c])):
            for s in range(-3, 4):
                if s > 0:
                    w = pltpu.roll(jnp.where(lane < s, e, v), 128 - s, 1)
                elif s < 0:
                    w = pltpu.roll(jnp.where(lane >= 128 + s, e, v), -s, 1)
                else:
                    w = v
                parts.append(w)
        halo = parts[TAPS:]
        pairs = [jnp.where(top, halo[p], halo[p + 1]) for p in (0, 2, 4)]
        cols.append(jnp.concatenate(parts[:TAPS] + pairs + [halo[6]], axis=0))
    return jnp.concatenate(cols, axis=1)


def block_kernel(
    x_hbm, h_hbm, cot_hbm, win_hbm, wout_hbm, fl, fr, kp, table, vec, bias,
    out_hbm, g_hbm, g1_ref, g2_ref, grad_ref,
    x_ref, hs, cot_ref, g_ref, win, wout, win_t, wout_t, vecs, bin_ref,
    edge, cv, ct, gv, rv, pre, ga, act, gp, nrm, gm, xh, inv, gwo, gwi,
    x_sem, h_sem, cot_sem, w_sem, out_sem, g_sem,
):
    lat = lax.axis_index("lat")
    streams = ((x_hbm, x_ref, x_sem), (h_hbm, hs, h_sem), (cot_hbm, cot_ref, cot_sem))
    for g in range(NG):
        for src, dst, sem in streams:
            group_copy(src, dst, sem, g).start()
    win_copy = pltpu.make_async_copy(win_hbm, win, w_sem.at[0])
    wout_copy = pltpu.make_async_copy(wout_hbm, wout_t, w_sem.at[1])
    win_copy.start()
    wout_copy.start()
    lane = lax.broadcasted_iota(jnp.int32, (ROWS, 128), 1)
    top = lax.broadcasted_iota(jnp.int32, (ROWS, 128), 0) < 8
    columns = jnp.transpose(vec[...])
    for k in range(5):
        vecs[k] = jnp.broadcast_to(columns[:, k : k + 1], (C, 128))
    cbias, gain, nbias, bout, scale = (vecs.at[k] for k in range(5))
    columns = jnp.transpose(bias[...])
    bin_ref[...] = jnp.broadcast_to(columns[:, 0:1], (HID, 128))
    spread_edges(fl, fr, edge)
    idx = table[lat]

    def conv_group(g, carry):
        for src, dst, sem in streams:
            group_copy(src, dst, sem, g).wait()
        for cc in range(GROUP):
            c = g * GROUP + cc
            col = shifted(x_ref, hs, edge, c, lane, top)
            r = jnp.dot(tap_tile(kp, idx, c), col, preferred_element_type=f32)
            r = r[:ROWS] + r[ROWS:]
            for m in range(M):
                cv[m, :, c, :] = r[:, m * 128 : (m + 1) * 128]
                ct[m, :, c, :] = cot_ref[m, c].astype(f32)
        return carry

    lax.fori_loop(0, NG, conv_group, 0)
    win_copy.wait()
    wout_copy.wait()
    win_t[...] = jnp.transpose(win[...])
    wout[...] = jnp.transpose(wout_t[...])
    gwo[...] = jnp.zeros_like(gwo)
    gwi[...] = jnp.zeros_like(gwi)

    def wide(ref):
        return jnp.concatenate([ref[...], ref[...]], axis=1)

    def rows_of(q):
        return q // 8, (q % 8) * 2

    def norm_steps(q, b):
        m, i = rows_of(q)
        conv = jnp.concatenate([cv[m, i, 0:C, :], cv[m, i + 1, 0:C, :]], axis=1) + wide(cbias)
        centred = conv - jnp.mean(conv, axis=0, keepdims=True)
        inv_std = lax.rsqrt(jnp.mean(centred * centred, axis=0, keepdims=True) + eps_norm)
        x_hat = centred * inv_std
        xh[b] = x_hat
        inv[b] = jnp.broadcast_to(inv_std, (8, CELLS))
        nrm[b] = (x_hat * wide(gain) + wide(nbias)).astype(bf16)
        gm[b] = (wide(scale) * jnp.concatenate([ct[m, i, 0:C, :], ct[m, i + 1, 0:C, :]], axis=1)).astype(bf16)
        yield
        pre[b] = jnp.dot(win_t[...], nrm[b], preferred_element_type=f32)
        yield
        ga[b] = jnp.dot(wout[...], gm[b], preferred_element_type=f32)
        yield

    def gelu_steps(b):
        for blk in range(HID // 32):
            s = pl.ds(blk * 32, 32)
            bias = bin_ref[s, :]
            p = pre[b, s, :] + jnp.concatenate([bias, bias], axis=1)
            phi = 0.5 * (1.0 + lax.erf(p * inv_root_two))
            act[b, s, :] = (p * phi).astype(bf16)
            slope = phi + p * jnp.exp(-0.5 * p * p) * inv_root_tau
            gp[b, s, :] = (ga[b, s, :] * slope).astype(bf16)
            yield

    def out_steps(q, b):
        m, i = rows_of(q)
        across = (((1,), (1,)), ((), ()))
        mlp = jnp.dot(wout_t[...], act[b], preferred_element_type=f32)
        res = wide(scale) * (mlp + wide(bout))
        rv[m, i, 0:C, :] = res[:, :128]
        rv[m, i + 1, 0:C, :] = res[:, 128:]
        yield
        g_hat = jnp.dot(win[...], gp[b], preferred_element_type=f32) * wide(gain)
        yield
        x_hat = xh[b]
        m1 = jnp.mean(g_hat, axis=0, keepdims=True)
        m2 = jnp.mean(g_hat * x_hat, axis=0, keepdims=True)
        g_conv = inv[b, 0:1, :] * (g_hat - m1 - x_hat * m2)
        gv[m, i, 0:C, :] = g_conv[:, :128]
        gv[m, i + 1, 0:C, :] = g_conv[:, 128:]
        yield
        gwo[...] += lax.dot_general(act[b], gm[b], across, preferred_element_type=f32)
        yield
        gwi[...] += lax.dot_general(gp[b], nrm[b], across, preferred_element_type=f32)
        yield

    def weave(gelu, others):
        share = HID // 32 // sum(n for _, n in others)
        for it, n in others:
            for _ in range(n):
                next(it, None)
                for _ in range(share):
                    next(gelu, None)
        for _ in gelu:
            pass
        for it, _ in others:
            for _ in it:
                pass

    for _ in norm_steps(0, 0):
        pass
    weave(gelu_steps(0), [(norm_steps(1, 1), 3)])

    def mlp_pair(j, carry):
        q = 2 * j + 1
        weave(gelu_steps(1), [(out_steps(q - 1, 0), 5), (norm_steps(q + 1, 0), 3)])
        weave(gelu_steps(0), [(out_steps(q, 1), 5), (norm_steps(q + 2, 1), 3)])
        return carry

    lax.fori_loop(0, 7, mlp_pair, 0)
    weave(gelu_steps(1), [(out_steps(14, 0), 5)])
    for _ in out_steps(15, 1):
        pass
    grad_ref[0:768, :] = gwo[:, 0:128].astype(bf16)
    grad_ref[768:1536, :] = gwi[:, 0:128].astype(bf16)
    grad_ref[1536:2304, :] = jnp.concatenate([gwo[:, 128:192], gwi[:, 128:192]], axis=1).astype(bf16)

    grad_ref[2304:FLAT, :] = jnp.zeros((FLAT - 2304, 128), bf16)
    even = lat % 2 == 0

    def out_group(g, carry):
        for cc in range(GROUP):
            c = g * GROUP + cc
            for m in range(M):
                tile = gv[m, :, c, :].astype(bf16)
                g_ref[m, c] = tile
                cot_ref[m, c] = (x_ref[m, c].astype(f32) + rv[m, :, c, :]).astype(bf16)
                low, high = tile[0:4], tile[12:16]
                g1_ref[m, c] = jnp.where(even, high, low)
                g2_ref[m, c] = jnp.where(even, low, high)
        group_copy(cot_ref, out_hbm, out_sem, g).start()
        group_copy(g_ref, g_hbm, g_sem, g).start()
        return carry

    lax.fori_loop(0, NG, out_group, 0)
    for g in range(NG):
        group_copy(cot_ref, out_hbm, out_sem, g).wait()
        group_copy(g_ref, g_hbm, g_sem, g).wait()


def tap_kernel(
    x_hbm, h_hbm, g_hbm, grads_in, fl, fr, diag_ref, grads_hbm,
    x_ref, hs, g_ref, edge, sums, x_sem, h_sem, g_sem, sum_sem,
):
    streams = ((x_hbm, x_ref, x_sem), (h_hbm, hs, h_sem), (g_hbm, g_ref, g_sem))
    for g in range(NG):
        for src, dst, sem in streams:
            group_copy(src, dst, sem, g).start()
    lat = lax.axis_index("lat")
    lane = lax.broadcasted_iota(jnp.int32, (ROWS, 128), 1)
    top = lax.broadcasted_iota(jnp.int32, (ROWS, 128), 0) < 8
    second = diag_ref[lat, 2] == 1
    blank = jnp.zeros((ROWS, 256 - DEPTH), f32)
    spread_edges(fl, fr, edge)

    def tap_group(g, carry):
        for src, dst, sem in streams:
            group_copy(src, dst, sem, g).wait()
        rows = []
        for cc in range(GROUP):
            c = g * GROUP + cc
            col = shifted(x_ref, hs, edge, c, lane, top)
            r = lax.dot_general(
                jnp.concatenate([g_ref[m, c] for m in range(M)], axis=1), col,
                (((1,), (1,)), ((), ())), preferred_element_type=f32,
            )
            d0 = jnp.take_along_axis(r[:, :128], diag_ref[lat, 0], axis=1)
            rest = jnp.concatenate([r[:, 128:], blank], axis=1)
            d1 = jnp.take_along_axis(rest, diag_ref[lat, 1], axis=1)
            d = jnp.where(second, d1, d0)
            rows.append(jnp.sum(d, axis=0, keepdims=True))
        start = pl.multiple_of(g * GROUP, GROUP)
        sums[pl.ds(start, GROUP), :] = jnp.concatenate(rows, axis=0).astype(bf16)
        return carry

    lax.fori_loop(0, NG, tap_group, 0)
    copy = pltpu.make_async_copy(sums, grads_hbm.at[pl.ds(2304, C)], sum_sem.at[0])
    copy.start()
    copy.wait()


def final_kernel(every, out_t, in_ref, taps):
    out_t[0:128, :] = jnp.transpose(every[0:768, :].astype(f32))
    in_ref[0:128, :] = jnp.transpose(every[768:1536, :].astype(f32))
    mixed = jnp.transpose(every[1536:2304, :].astype(f32))
    out_t[128:192, :] = mixed[0:64]
    in_ref[128:192, :] = mixed[64:128]
    sums = jnp.transpose(every[2304:2496, :].astype(f32))
    for a in range(TAPS):
        taps[a] = sums[a * 8 : a * 8 + TAPS]


def back_kernel(
    x_hbm, h_hbm, cot_hbm, fl, fr, kp, table, out_hbm,
    g_ref, hs, cot_ref, edge, x_sem, h_sem, cot_sem, out_sem,
):
    streams = ((x_hbm, g_ref, x_sem), (h_hbm, hs, h_sem), (cot_hbm, cot_ref, cot_sem))
    for g in range(NG):
        for src, dst, sem in streams:
            group_copy(src, dst, sem, g).start()
    lane = lax.broadcasted_iota(jnp.int32, (ROWS, 128), 1)
    top = lax.broadcasted_iota(jnp.int32, (ROWS, 128), 0) < 8
    spread_edges(fl, fr, edge)
    idx = table[lax.axis_index("lat")]

    def group(g, carry):
        for src, dst, sem in streams:
            group_copy(src, dst, sem, g).wait()
        for cc in range(GROUP):
            c = g * GROUP + cc
            col = shifted(g_ref, hs, edge, c, lane, top)
            r = jnp.dot(tap_tile(kp, idx, c), col, preferred_element_type=f32)
            r = r[:ROWS] + r[ROWS:]
            for m in range(M):
                back = r[:, m * 128 : (m + 1) * 128]
                cot_ref[m, c] = (cot_ref[m, c].astype(f32) + back).astype(bf16)
        group_copy(cot_ref, out_hbm, out_sem, g).start()
        return carry

    lax.fori_loop(0, NG, group, 0)
    for g in range(NG):
        group_copy(cot_ref, out_hbm, out_sem, g).wait()


EDGE = pltpu.VMEM((2, M, C, ROWS, LON), bf16)
TILES = pltpu.VMEM((M, C, ROWS, LON), bf16)
SEMS = pltpu.SemaphoreType.DMA((NG,))
ANY = pl.BlockSpec(memory_space=pl.ANY)
VMEM = pl.BlockSpec(memory_space=pltpu.VMEM)
BLOCK_SCRATCH = [
    TILES,
    TILES,
    TILES,
    TILES,
    pltpu.VMEM((C, HID), bf16),
    pltpu.VMEM((HID, C), bf16),
    pltpu.VMEM((HID, C), bf16),
    pltpu.VMEM((C, HID), bf16),
    pltpu.VMEM((5, C, 128), f32),
    pltpu.VMEM((HID, 128), f32),
    EDGE,
    pltpu.VMEM((M, ROWS, PITCH, LON), f32),
    pltpu.VMEM((M, ROWS, PITCH, LON), f32),
    pltpu.VMEM((M, ROWS, PITCH, LON), f32),
    pltpu.VMEM((M, ROWS, PITCH, LON), f32),
    pltpu.VMEM((2, HID, CELLS), f32),
    pltpu.VMEM((2, HID, CELLS), f32),
    pltpu.VMEM((2, HID, CELLS), bf16),
    pltpu.VMEM((2, HID, CELLS), bf16),
    pltpu.VMEM((2, C, CELLS), bf16),
    pltpu.VMEM((2, C, CELLS), bf16),
    pltpu.VMEM((2, C, CELLS), f32),
    pltpu.VMEM((2, 8, CELLS), f32),
    pltpu.VMEM((HID, C), f32),
    pltpu.VMEM((HID, C), f32),
    SEMS,
    SEMS,
    SEMS,
    pltpu.SemaphoreType.DMA((2,)),
    SEMS,
    SEMS,
]


def routes():
    def flat(lat, lon):
        return lat * N_LON + lon % N_LON

    first = {0: (1, 0), 1: (0, 0), 2: (3, 0), 3: (2, 0)}
    second = {0: (0, 16), 1: (2, 0), 2: (1, 0), 3: (3, 16)}
    return [
        [
            (flat(lat, lon), flat(step[lat][0], lon + step[lat][1]))
            for lat in range(N_LAT)
            for lon in range(N_LON)
        ]
        for step in (first, second)
    ]


def exchange_rows(first, second):
    p1, p2 = routes()
    both = ("lat", "lon")
    return lax.ppermute(first, both, p1), lax.ppermute(second, both, p2)


def own_pack(x):
    own = jax.ShapeDtypeStruct((M * NG, ROWS, LON), bf16)
    return pl.pallas_call(
        own_pack_kernel, out_shape=(own, own), compiler_params=SMALL, name="own_pack"
    )(x)


def halo_pack(r1, r2, right, left):
    packed = jax.ShapeDtypeStruct((M * NG, 2 * ROWS, LON), bf16)
    return pl.pallas_call(
        halo_pack_kernel,
        out_shape=(jax.ShapeDtypeStruct((M, C, ROWS, LON), bf16), packed, packed),
        compiler_params=SMALL,
        name="halo_pack",
    )(r1, r2, right, left)


def tap_sums(x, hs, g_round, from_left, from_right, grads):
    return pl.pallas_call(
        tap_kernel,
        out_shape=jax.ShapeDtypeStruct((FLAT, 128), bf16),
        in_specs=[ANY] * 4 + [VMEM] * 3,
        out_specs=ANY,
        scratch_shapes=[
            TILES, TILES, TILES, EDGE, pltpu.VMEM((C, 128), bf16),
            SEMS, SEMS, SEMS, pltpu.SemaphoreType.DMA((1,)),
        ],
        input_output_aliases={3: 0},
        compiler_params=PARAMS,
        name="tap_sums",
    )(x, hs, g_round, grads, from_left, from_right, DIAG_TABLE)


def exchange_cols(right, left):
    forward = [(i, (i + 1) % N_LON) for i in range(N_LON)]
    backward = [(t, s) for s, t in forward]
    return lax.ppermute(right, "lon", forward), lax.ppermute(left, "lon", backward)


def shards(
    inputs, cotangent, kernel, conv_bias, norm_gain, norm_bias,
    w_in, bias_in, w_out, bias_out, layer_scale,
):
    both = ("lat", "lon")
    even = lax.axis_index("lat") % 2 == 0
    tile = jax.ShapeDtypeStruct((M, C, ROWS, LON), bf16)
    taps = jnp.pad(jnp.swapaxes(kernel, 1, 2), ((0, 0), (0, 0), (0, 1)))
    taps = jnp.pad(taps.reshape(C, 56), ((0, 0), (0, 72)))
    rows = (conv_bias, norm_gain, norm_bias, bias_out, layer_scale)
    low, high = inputs[:, :, :4], inputs[:, :, 12:]
    r1, r2 = exchange_rows(jnp.where(even, high, low), jnp.where(even, low, high))
    vec = jnp.stack(rows + rows[:3])
    bias = jnp.broadcast_to(bias_in[None], (8, HID))
    r1, r2, own, taps, vec, bias = lax.optimization_barrier(
        (r1, r2, own_pack(inputs), taps, vec, bias)
    )
    hs, right, left = halo_pack(r1, r2, *own)
    x_cols = exchange_cols(right, left)
    edge_rows = jax.ShapeDtypeStruct((M, C, 4, LON), bf16)
    output, g_round, g1, g2, grads = pl.pallas_call(
        block_kernel,
        out_shape=(tile, tile, edge_rows, edge_rows, jax.ShapeDtypeStruct((FLAT, 128), bf16)),
        in_specs=[ANY] * 5 + [VMEM] * 6,
        out_specs=(ANY, ANY, VMEM, VMEM, VMEM),
        scratch_shapes=BLOCK_SCRATCH,
        compiler_params=PARAMS,
        name="block",
    )(
        inputs, hs, cotangent, w_in, w_out.T, *x_cols, taps, FWD_TABLE, vec, bias,
    )
    g1, g2, own, grads = lax.optimization_barrier(
        (
            *exchange_rows(g1, g2),
            own_pack(g_round),
            tap_sums(inputs, hs, g_round, *x_cols, grads),
        )
    )
    parts = lax.all_to_all(grads.reshape(128, CHUNK_ROWS, 128), both, 0, 0, tiled=True)
    g_halo, g_right, g_left = halo_pack(g1, g2, *own)
    factor = 1.0 / math.sqrt(M * ROWS * N_LAT * LON * N_LON)
    mine = (jnp.sum(parts.astype(f32), axis=0) * factor).astype(bf16)
    mine, g_cols = lax.optimization_barrier((mine, exchange_cols(g_right, g_left)))
    grad_input = pl.pallas_call(
        back_kernel,
        out_shape=tile,
        in_specs=[ANY] * 3 + [VMEM] * 4,
        out_specs=ANY,
        scratch_shapes=[TILES, TILES, TILES, EDGE, SEMS, SEMS, SEMS, SEMS],
        compiler_params=PARAMS,
        name="back",
    )(g_round, g_halo, cotangent, *g_cols, taps, SPR_TABLE)
    every = lax.all_to_all(
        jnp.broadcast_to(mine[None], (128, CHUNK_ROWS, 128)), both, 0, 0, tiled=True
    ).reshape(FLAT, 128)
    grad_out, grad_in, grad_kernel = pl.pallas_call(
        final_kernel,
        out_shape=(
            jax.ShapeDtypeStruct((C, HID), f32),
            jax.ShapeDtypeStruct((C, HID), f32),
            jax.ShapeDtypeStruct((TAPS, TAPS, C), f32),
        ),
        compiler_params=SMALL,
        name="final",
    )(every)
    grad_out = grad_out.T
    grad_kernel = jnp.transpose(grad_kernel, (2, 0, 1))
    return output, grad_input, grad_kernel, grad_in, grad_out


def solution(mesh):
    placed = (P(None, None, "lat", "lon"),) * 2 + (P(),) * 9
    return jax.shard_map(
        shards,
        mesh=mesh,
        in_specs=placed,
        out_specs=(P(None, None, "lat", "lon"),) * 2 + (P(),) * 3,
        check_vma=False,
    )
```

```python
import math

import jax
import jax.numpy as jnp
import numpy as np
from jax import lax
from jax.experimental import pallas as pl
from jax.experimental.pallas import tpu as pltpu
from jax.sharding import PartitionSpec as P

eps_norm = 1e-06
inv_root_two = 0.7071067811865476
inv_root_tau = 0.3989422804014327
f32 = jnp.float32
bf16 = jnp.bfloat16

M, C, HID, ROWS, LON = 2, 192, 768, 16, 128
GROUP = 32
NG = C // GROUP
TAPS = 7
OWN_K = TAPS * 16
DEPTH = OWN_K + 64
N_LAT, N_LON = 4, 32
PITCH = C + 8
CELLS = 256
CHUNK_ROWS = 24
FLAT = 128 * CHUNK_ROWS
PARAMS = pltpu.CompilerParams(vmem_limit_bytes=60 * 2**20)
MIDDLE = pltpu.CompilerParams(vmem_limit_bytes=52 * 2**20)
SMALL = pltpu.CompilerParams(vmem_limit_bytes=16 * 2**20)


def halo_row(lat, pos):
    half, k = divmod(pos, 4)
    if lat == 0:
        return 16 + k if half == 0 else -1 - k
    if lat == 1:
        return k - 4 if half == 0 else 16 + k
    if lat == 2:
        return 16 + k if half == 0 else k - 4
    return k - 4 if half == 0 else 19 - k


def tap_tables():
    fwd = np.full((N_LAT, ROWS, 256), 127, np.int32)
    spr = np.full((N_LAT, ROWS, 256), 127, np.int32)
    diag = np.zeros((N_LAT, 3, ROWS, 128), np.int32)
    for lat in range(N_LAT):
        for i in range(ROWS):
            for t in range(TAPS):
                for pos in range(24):
                    k = pos % 4
                    row = pos - 8 if pos >= 8 else halo_row(lat, pos)
                    a_fwd = row - i + 3
                    a_spr = i - row + 3
                    if lat == 0 and 4 <= pos < 8:
                        a_spr = 2 - i - k
                    if lat == 3 and 4 <= pos < 8:
                        a_spr = 22 - i - k
                    if pos >= 8:
                        source = t * 16 + pos - 8
                    else:
                        source = OWN_K + t * 8 + pos
                    if 0 <= a_fwd < TAPS:
                        fwd[lat, i, source] = t * 8 + a_fwd
                        diag[lat, source // 128, i, a_fwd * 8 + t] = source % 128
                        diag[lat, 2, i, a_fwd * 8 + t] = source // 128
                    if 0 <= a_spr < TAPS:
                        spr[lat, i, source] = (6 - t) * 8 + a_spr
    return fwd, spr, diag


FWD_TABLE, SPR_TABLE, DIAG_TABLE = tap_tables()


def pick(cc, transposed):
    shape = (128, 256) if transposed else (256, 128)
    packed = lax.broadcasted_iota(jnp.int32, shape, 1 if transposed else 0)
    lane = lax.broadcasted_iota(jnp.int32, shape, 0 if transposed else 1)
    k = packed % 128 - 4 * cc
    hit = (k >= 0) & (k < 3) & (lane == k + jnp.where(packed < 128, 125, 0))
    return jnp.where(hit, 1.0, 0.0).astype(bf16)


def own_pack_kernel(x_ref, right_ref, left_ref):
    total = jnp.zeros((M * NG * ROWS, 256), f32)
    for cc in range(0, GROUP, 2):
        total = total + edge_product(x_ref, cc)
    packed = total.astype(bf16).reshape(M * NG, ROWS, 256)
    right_ref[...] = packed[:, :, :128]
    left_ref[...] = packed[:, :, 128:]


def edge_product(x_ref, cc):
    lhs = jnp.concatenate(
        [
            jnp.concatenate(
                [x_ref[m, g * GROUP + cc + d] for m in range(M) for g in range(NG)], axis=0
            )
            for d in range(2)
        ],
        axis=1,
    )
    rhs = jnp.concatenate([pick(cc, True), pick(cc + 1, True)], axis=0)
    return jnp.dot(lhs, rhs, preferred_element_type=f32)


def halo_pack_kernel(r1, r2, own_right, own_left, hs, right_ref, left_ref):
    def channel(c, carry):
        for m in range(M):
            hs[m, c] = jnp.concatenate([r1[m, c], r2[m, c], r1[m, c], r2[m, c]], axis=0)
        return carry

    lax.fori_loop(0, C, channel, 0, unroll=8)
    total = jnp.zeros((M * NG * ROWS, 256), f32)
    for cc in range(0, GROUP, 2):
        total = total + edge_product(hs, cc)
    packed = total.astype(bf16).reshape(M * NG, ROWS, 256)
    right_ref[:, 0:ROWS, :] = own_right[...]
    left_ref[:, 0:ROWS, :] = own_left[...]
    right_ref[:, ROWS : 2 * ROWS, :] = packed[:, :, :128]
    left_ref[:, ROWS : 2 * ROWS, :] = packed[:, :, 128:]


def spread_edges(from_left, from_right, edge):
    lhs = jnp.concatenate(
        [
            jnp.concatenate(
                [ref[q, k * ROWS : (k + 1) * ROWS, :] for k in range(2) for q in range(M * NG)],
                axis=0,
            )
            for ref in (from_left, from_right)
        ],
        axis=1,
    )
    for cc in range(0, GROUP, 2):
        rhs = jnp.concatenate([pick(cc, False), pick(cc + 1, False)], axis=1)
        tiles = jnp.dot(lhs, rhs, preferred_element_type=f32).astype(bf16)
        for d in range(2):
            part = tiles[:, d * 128 : (d + 1) * 128].reshape(2, M * NG, ROWS, 128)
            for k in range(2):
                for q in range(M * NG):
                    edge[k, q // NG, (q % NG) * GROUP + cc + d] = part[k, q]


def tap_tile(kp, idx, c):
    row = jnp.broadcast_to(kp[pl.ds(c, 1), :], (ROWS, 128))
    taps = jnp.concatenate(
        [
            jnp.take_along_axis(row, idx[:, :128], axis=1),
            jnp.take_along_axis(row, idx[:, 128:], axis=1),
        ],
        axis=1,
    )
    high = taps.astype(bf16)
    both = jnp.concatenate([high, (taps - high.astype(f32)).astype(bf16)], axis=0)
    return both[:, :DEPTH]


def group_copy(src, dst, sem, g):
    part = pl.ds(pl.multiple_of(g * GROUP, GROUP), GROUP)
    return pltpu.make_async_copy(src.at[:, part], dst.at[:, part], sem.at[g])


def shifted(x_ref, hs, edge, c, lane, top):
    cols = []
    for m in range(M):
        parts = []
        for v, e in ((x_ref[m, c], edge[0, m, c]), (hs[m, c], edge[1, m, c])):
            for s in range(-3, 4):
                if s > 0:
                    w = pltpu.roll(jnp.where(lane < s, e, v), 128 - s, 1)
                elif s < 0:
                    w = pltpu.roll(jnp.where(lane >= 128 + s, e, v), -s, 1)
                else:
                    w = v
                parts.append(w)
        halo = parts[TAPS:]
        pairs = [jnp.where(top, halo[p], halo[p + 1]) for p in (0, 2, 4)]
        cols.append(jnp.concatenate(parts[:TAPS] + pairs + [halo[6]], axis=0))
    return jnp.concatenate(cols, axis=1)


def block_kernel(
    x_hbm, h_hbm, cot_hbm, win_hbm, wout_hbm, fl, fr, kp, table, vec, bias,
    out_hbm, g_hbm, g1_ref, g2_ref, grad_ref,
    x_ref, hs, cot_ref, g_ref, win, wout, win_t, wout_t, vecs, bin_ref,
    edge, cv, ct, gv, rv, pre, ga, act, gp, nrm, gm, xh, inv, gwo, gwi,
    x_sem, h_sem, cot_sem, w_sem, out_sem, g_sem,
):
    lat = lax.axis_index("lat")
    streams = ((x_hbm, x_ref, x_sem), (h_hbm, hs, h_sem), (cot_hbm, cot_ref, cot_sem))
    for g in range(NG):
        for src, dst, sem in streams:
            group_copy(src, dst, sem, g).start()
    win_copy = pltpu.make_async_copy(win_hbm, win, w_sem.at[0])
    wout_copy = pltpu.make_async_copy(wout_hbm, wout_t, w_sem.at[1])
    win_copy.start()
    wout_copy.start()
    lane = lax.broadcasted_iota(jnp.int32, (ROWS, 128), 1)
    top = lax.broadcasted_iota(jnp.int32, (ROWS, 128), 0) < 8
    columns = jnp.transpose(vec[...])
    for k in range(5):
        vecs[k] = jnp.broadcast_to(columns[:, k : k + 1], (C, 128))
    cbias, gain, nbias, bout, scale = (vecs.at[k] for k in range(5))
    columns = jnp.transpose(bias[...])
    bin_ref[...] = jnp.broadcast_to(columns[:, 0:1], (HID, 128))
    spread_edges(fl, fr, edge)
    idx = table[lat]

    def conv_group(g, carry):
        for src, dst, sem in streams:
            group_copy(src, dst, sem, g).wait()
        for cc in range(GROUP):
            c = g * GROUP + cc
            col = shifted(x_ref, hs, edge, c, lane, top)
            r = jnp.dot(tap_tile(kp, idx, c), col, preferred_element_type=f32)
            r = r[:ROWS] + r[ROWS:]
            for m in range(M):
                cv[m, :, c, :] = r[:, m * 128 : (m + 1) * 128]
                ct[m, :, c, :] = cot_ref[m, c].astype(f32)
        return carry

    lax.fori_loop(0, NG, conv_group, 0)
    win_copy.wait()
    wout_copy.wait()
    win_t[...] = jnp.transpose(win[...])
    wout[...] = jnp.transpose(wout_t[...])
    gwo[...] = jnp.zeros_like(gwo)
    gwi[...] = jnp.zeros_like(gwi)

    def wide(ref):
        return jnp.concatenate([ref[...], ref[...]], axis=1)

    def rows_of(q):
        return q // 8, (q % 8) * 2

    def norm_steps(q, b):
        m, i = rows_of(q)
        conv = jnp.concatenate([cv[m, i, 0:C, :], cv[m, i + 1, 0:C, :]], axis=1) + wide(cbias)
        centred = conv - jnp.mean(conv, axis=0, keepdims=True)
        inv_std = lax.rsqrt(jnp.mean(centred * centred, axis=0, keepdims=True) + eps_norm)
        x_hat = centred * inv_std
        xh[b] = x_hat
        inv[b] = jnp.broadcast_to(inv_std, (8, CELLS))
        nrm[b] = (x_hat * wide(gain) + wide(nbias)).astype(bf16)
        gm[b] = (wide(scale) * jnp.concatenate([ct[m, i, 0:C, :], ct[m, i + 1, 0:C, :]], axis=1)).astype(bf16)
        yield
        pre[b] = jnp.dot(win_t[...], nrm[b], preferred_element_type=f32)
        yield
        ga[b] = jnp.dot(wout[...], gm[b], preferred_element_type=f32)
        yield

    def gelu_steps(b):
        for blk in range(HID // 32):
            s = pl.ds(blk * 32, 32)
            bias = bin_ref[s, :]
            p = pre[b, s, :] + jnp.concatenate([bias, bias], axis=1)
            phi = 0.5 * (1.0 + lax.erf(p * inv_root_two))
            act[b, s, :] = (p * phi).astype(bf16)
            slope = phi + p * jnp.exp(-0.5 * p * p) * inv_root_tau
            gp[b, s, :] = (ga[b, s, :] * slope).astype(bf16)
            yield

    def out_steps(q, b):
        m, i = rows_of(q)
        across = (((1,), (1,)), ((), ()))
        mlp = jnp.dot(wout_t[...], act[b], preferred_element_type=f32)
        res = wide(scale) * (mlp + wide(bout))
        rv[m, i, 0:C, :] = res[:, :128]
        rv[m, i + 1, 0:C, :] = res[:, 128:]
        yield
        g_hat = jnp.dot(win[...], gp[b], preferred_element_type=f32) * wide(gain)
        yield
        x_hat = xh[b]
        m1 = jnp.mean(g_hat, axis=0, keepdims=True)
        m2 = jnp.mean(g_hat * x_hat, axis=0, keepdims=True)
        g_conv = inv[b, 0:1, :] * (g_hat - m1 - x_hat * m2)
        gv[m, i, 0:C, :] = g_conv[:, :128]
        gv[m, i + 1, 0:C, :] = g_conv[:, 128:]
        yield
        gwo[...] += lax.dot_general(act[b], gm[b], across, preferred_element_type=f32)
        yield
        gwi[...] += lax.dot_general(gp[b], nrm[b], across, preferred_element_type=f32)
        yield

    def weave(gelu, others):
        share = HID // 32 // sum(n for _, n in others)
        for it, n in others:
            for _ in range(n):
                next(it, None)
                for _ in range(share):
                    next(gelu, None)
        for _ in gelu:
            pass
        for it, _ in others:
            for _ in it:
                pass

    for _ in norm_steps(0, 0):
        pass
    weave(gelu_steps(0), [(norm_steps(1, 1), 3)])

    def mlp_pair(j, carry):
        q = 2 * j + 1
        weave(gelu_steps(1), [(out_steps(q - 1, 0), 5), (norm_steps(q + 1, 0), 3)])
        weave(gelu_steps(0), [(out_steps(q, 1), 5), (norm_steps(q + 2, 1), 3)])
        return carry

    lax.fori_loop(0, 7, mlp_pair, 0)
    weave(gelu_steps(1), [(out_steps(14, 0), 5)])
    for _ in out_steps(15, 1):
        pass
    grad_ref[0:768, :] = gwo[:, 0:128].astype(bf16)
    grad_ref[768:1536, :] = gwi[:, 0:128].astype(bf16)
    grad_ref[1536:2304, :] = jnp.concatenate([gwo[:, 128:192], gwi[:, 128:192]], axis=1).astype(bf16)

    grad_ref[2304:FLAT, :] = jnp.zeros((FLAT - 2304, 128), bf16)
    even = lat % 2 == 0

    def out_group(g, carry):
        for cc in range(GROUP):
            c = g * GROUP + cc
            for m in range(M):
                tile = gv[m, :, c, :].astype(bf16)
                g_ref[m, c] = tile
                cot_ref[m, c] = (x_ref[m, c].astype(f32) + rv[m, :, c, :]).astype(bf16)
                low, high = tile[0:4], tile[12:16]
                g1_ref[m, c] = jnp.where(even, high, low)
                g2_ref[m, c] = jnp.where(even, low, high)
        group_copy(cot_ref, out_hbm, out_sem, g).start()
        group_copy(g_ref, g_hbm, g_sem, g).start()
        return carry

    lax.fori_loop(0, NG, out_group, 0)
    for g in range(NG):
        group_copy(cot_ref, out_hbm, out_sem, g).wait()
        group_copy(g_ref, g_hbm, g_sem, g).wait()


def tap_kernel(
    x_hbm, h_hbm, g_hbm, grads_in, fl, fr, diag_ref, grads_hbm,
    x_ref, hs, g_ref, edge, sums, x_sem, h_sem, g_sem, sum_sem,
):
    streams = ((x_hbm, x_ref, x_sem), (h_hbm, hs, h_sem), (g_hbm, g_ref, g_sem))
    for g in range(NG):
        for src, dst, sem in streams:
            group_copy(src, dst, sem, g).start()
    lat = lax.axis_index("lat")
    lane = lax.broadcasted_iota(jnp.int32, (ROWS, 128), 1)
    top = lax.broadcasted_iota(jnp.int32, (ROWS, 128), 0) < 8
    second = diag_ref[lat, 2] == 1
    blank = jnp.zeros((ROWS, 256 - DEPTH), f32)
    spread_edges(fl, fr, edge)

    def tap_group(g, carry):
        for src, dst, sem in streams:
            group_copy(src, dst, sem, g).wait()
        rows = []
        for cc in range(GROUP):
            c = g * GROUP + cc
            col = shifted(x_ref, hs, edge, c, lane, top)
            r = lax.dot_general(
                jnp.concatenate([g_ref[m, c] for m in range(M)], axis=1), col,
                (((1,), (1,)), ((), ())), preferred_element_type=f32,
            )
            d0 = jnp.take_along_axis(r[:, :128], diag_ref[lat, 0], axis=1)
            rest = jnp.concatenate([r[:, 128:], blank], axis=1)
            d1 = jnp.take_along_axis(rest, diag_ref[lat, 1], axis=1)
            d = jnp.where(second, d1, d0)
            rows.append(jnp.sum(d, axis=0, keepdims=True))
        start = pl.multiple_of(g * GROUP, GROUP)
        sums[pl.ds(start, GROUP), :] = jnp.concatenate(rows, axis=0).astype(bf16)
        return carry

    lax.fori_loop(0, NG, tap_group, 0)
    copy = pltpu.make_async_copy(sums, grads_hbm.at[pl.ds(2304, C)], sum_sem.at[0])
    copy.start()
    copy.wait()


def final_kernel(every, out_t, in_ref, taps):
    out_t[0:128, :] = jnp.transpose(every[0:768, :].astype(f32))
    in_ref[0:128, :] = jnp.transpose(every[768:1536, :].astype(f32))
    mixed = jnp.transpose(every[1536:2304, :].astype(f32))
    out_t[128:192, :] = mixed[0:64]
    in_ref[128:192, :] = mixed[64:128]
    sums = jnp.transpose(every[2304:2496, :].astype(f32))
    for a in range(TAPS):
        taps[a] = sums[a * 8 : a * 8 + TAPS]


def back_kernel(
    x_hbm, h_hbm, cot_hbm, fl, fr, kp, table, out_hbm,
    g_ref, hs, cot_ref, edge, x_sem, h_sem, cot_sem, out_sem,
):
    streams = ((x_hbm, g_ref, x_sem), (h_hbm, hs, h_sem), (cot_hbm, cot_ref, cot_sem))
    for g in range(NG):
        for src, dst, sem in streams:
            group_copy(src, dst, sem, g).start()
    lane = lax.broadcasted_iota(jnp.int32, (ROWS, 128), 1)
    top = lax.broadcasted_iota(jnp.int32, (ROWS, 128), 0) < 8
    spread_edges(fl, fr, edge)
    idx = table[lax.axis_index("lat")]

    def group(g, carry):
        for src, dst, sem in streams:
            group_copy(src, dst, sem, g).wait()
        for cc in range(GROUP):
            c = g * GROUP + cc
            col = shifted(g_ref, hs, edge, c, lane, top)
            r = jnp.dot(tap_tile(kp, idx, c), col, preferred_element_type=f32)
            r = r[:ROWS] + r[ROWS:]
            for m in range(M):
                back = r[:, m * 128 : (m + 1) * 128]
                cot_ref[m, c] = (cot_ref[m, c].astype(f32) + back).astype(bf16)
        group_copy(cot_ref, out_hbm, out_sem, g).start()
        return carry

    lax.fori_loop(0, NG, group, 0)
    for g in range(NG):
        group_copy(cot_ref, out_hbm, out_sem, g).wait()


EDGE = pltpu.VMEM((2, M, C, ROWS, LON), bf16)
TILES = pltpu.VMEM((M, C, ROWS, LON), bf16)
SEMS = pltpu.SemaphoreType.DMA((NG,))
ANY = pl.BlockSpec(memory_space=pl.ANY)
VMEM = pl.BlockSpec(memory_space=pltpu.VMEM)
BLOCK_SCRATCH = [
    TILES,
    TILES,
    TILES,
    TILES,
    pltpu.VMEM((C, HID), bf16),
    pltpu.VMEM((HID, C), bf16),
    pltpu.VMEM((HID, C), bf16),
    pltpu.VMEM((C, HID), bf16),
    pltpu.VMEM((5, C, 128), f32),
    pltpu.VMEM((HID, 128), f32),
    EDGE,
    pltpu.VMEM((M, ROWS, PITCH, LON), f32),
    pltpu.VMEM((M, ROWS, PITCH, LON), f32),
    pltpu.VMEM((M, ROWS, PITCH, LON), f32),
    pltpu.VMEM((M, ROWS, PITCH, LON), f32),
    pltpu.VMEM((2, HID, CELLS), f32),
    pltpu.VMEM((2, HID, CELLS), f32),
    pltpu.VMEM((2, HID, CELLS), bf16),
    pltpu.VMEM((2, HID, CELLS), bf16),
    pltpu.VMEM((2, C, CELLS), bf16),
    pltpu.VMEM((2, C, CELLS), bf16),
    pltpu.VMEM((2, C, CELLS), f32),
    pltpu.VMEM((2, 8, CELLS), f32),
    pltpu.VMEM((HID, C), f32),
    pltpu.VMEM((HID, C), f32),
    SEMS,
    SEMS,
    SEMS,
    pltpu.SemaphoreType.DMA((2,)),
    SEMS,
    SEMS,
]


def routes():
    def flat(lat, lon):
        return lat * N_LON + lon % N_LON

    first = {0: (1, 0), 1: (0, 0), 2: (3, 0), 3: (2, 0)}
    second = {0: (0, 16), 1: (2, 0), 2: (1, 0), 3: (3, 16)}
    return [
        [
            (flat(lat, lon), flat(step[lat][0], lon + step[lat][1]))
            for lat in range(N_LAT)
            for lon in range(N_LON)
        ]
        for step in (first, second)
    ]


def exchange_rows(first, second):
    p1, p2 = routes()
    both = ("lat", "lon")
    return lax.ppermute(first, both, p1), lax.ppermute(second, both, p2)


def own_pack(x):
    own = jax.ShapeDtypeStruct((M * NG, ROWS, LON), bf16)
    return pl.pallas_call(
        own_pack_kernel, out_shape=(own, own), compiler_params=SMALL, name="own_pack"
    )(x)


def halo_pack(r1, r2, right, left):
    packed = jax.ShapeDtypeStruct((M * NG, 2 * ROWS, LON), bf16)
    return pl.pallas_call(
        halo_pack_kernel,
        out_shape=(jax.ShapeDtypeStruct((M, C, ROWS, LON), bf16), packed, packed),
        compiler_params=MIDDLE,
        name="halo_pack",
    )(r1, r2, right, left)


def tap_sums(x, hs, g_round, from_left, from_right, grads):
    return pl.pallas_call(
        tap_kernel,
        out_shape=jax.ShapeDtypeStruct((FLAT, 128), bf16),
        in_specs=[ANY] * 4 + [VMEM] * 3,
        out_specs=ANY,
        scratch_shapes=[
            TILES, TILES, TILES, EDGE, pltpu.VMEM((C, 128), bf16),
            SEMS, SEMS, SEMS, pltpu.SemaphoreType.DMA((1,)),
        ],
        input_output_aliases={3: 0},
        compiler_params=PARAMS,
        name="tap_sums",
    )(x, hs, g_round, grads, from_left, from_right, DIAG_TABLE)


def exchange_cols(right, left):
    forward = [(i, (i + 1) % N_LON) for i in range(N_LON)]
    backward = [(t, s) for s, t in forward]
    return lax.ppermute(right, "lon", forward), lax.ppermute(left, "lon", backward)


def shards(
    inputs, cotangent, kernel, conv_bias, norm_gain, norm_bias,
    w_in, bias_in, w_out, bias_out, layer_scale,
):
    both = ("lat", "lon")
    even = lax.axis_index("lat") % 2 == 0
    tile = jax.ShapeDtypeStruct((M, C, ROWS, LON), bf16)
    taps = jnp.pad(jnp.swapaxes(kernel, 1, 2), ((0, 0), (0, 0), (0, 1)))
    taps = jnp.pad(taps.reshape(C, 56), ((0, 0), (0, 72)))
    rows = (conv_bias, norm_gain, norm_bias, bias_out, layer_scale)
    low, high = inputs[:, :, :4], inputs[:, :, 12:]
    r1, r2 = exchange_rows(jnp.where(even, high, low), jnp.where(even, low, high))
    vec = jnp.stack(rows + rows[:3])
    bias = jnp.broadcast_to(bias_in[None], (8, HID))
    r1, r2, own, taps, vec, bias = lax.optimization_barrier(
        (r1, r2, own_pack(inputs), taps, vec, bias)
    )
    hs, right, left = halo_pack(r1, r2, *own)
    x_cols = exchange_cols(right, left)
    edge_rows = jax.ShapeDtypeStruct((M, C, 4, LON), bf16)
    output, g_round, g1, g2, grads = pl.pallas_call(
        block_kernel,
        out_shape=(tile, tile, edge_rows, edge_rows, jax.ShapeDtypeStruct((FLAT, 128), bf16)),
        in_specs=[ANY] * 5 + [VMEM] * 6,
        out_specs=(ANY, ANY, VMEM, VMEM, VMEM),
        scratch_shapes=BLOCK_SCRATCH,
        compiler_params=PARAMS,
        name="block",
    )(
        inputs, hs, cotangent, w_in, w_out.T, *x_cols, taps, FWD_TABLE, vec, bias,
    )
    g1, g2, own, grads = lax.optimization_barrier(
        (
            *exchange_rows(g1, g2),
            own_pack(g_round),
            tap_sums(inputs, hs, g_round, *x_cols, grads),
        )
    )
    parts = lax.all_to_all(grads.reshape(128, CHUNK_ROWS, 128), both, 0, 0, tiled=True)
    g_halo, g_right, g_left = halo_pack(g1, g2, *own)
    factor = 1.0 / math.sqrt(M * ROWS * N_LAT * LON * N_LON)
    mine = (jnp.sum(parts.astype(f32), axis=0) * factor).astype(bf16)
    mine, g_cols = lax.optimization_barrier((mine, exchange_cols(g_right, g_left)))
    grad_input = pl.pallas_call(
        back_kernel,
        out_shape=tile,
        in_specs=[ANY] * 3 + [VMEM] * 4,
        out_specs=ANY,
        scratch_shapes=[TILES, TILES, TILES, EDGE, SEMS, SEMS, SEMS, SEMS],
        compiler_params=PARAMS,
        name="back",
    )(g_round, g_halo, cotangent, *g_cols, taps, SPR_TABLE)
    every = lax.all_to_all(
        jnp.broadcast_to(mine[None], (128, CHUNK_ROWS, 128)), both, 0, 0, tiled=True
    ).reshape(FLAT, 128)
    grad_out, grad_in, grad_kernel = pl.pallas_call(
        final_kernel,
        out_shape=(
            jax.ShapeDtypeStruct((C, HID), f32),
            jax.ShapeDtypeStruct((C, HID), f32),
            jax.ShapeDtypeStruct((TAPS, TAPS, C), f32),
        ),
        compiler_params=SMALL,
        name="final",
    )(every)
    grad_out = grad_out.T
    grad_kernel = jnp.transpose(grad_kernel, (2, 0, 1))
    return output, grad_input, grad_kernel, grad_in, grad_out


def solution(mesh):
    placed = (P(None, None, "lat", "lon"),) * 2 + (P(),) * 9
    return jax.shard_map(
        shards,
        mesh=mesh,
        in_specs=placed,
        out_specs=(P(None, None, "lat", "lon"),) * 2 + (P(),) * 3,
        check_vma=False,
    )
```
